768 devices in a mesh: grp: 48 (over z, x), intra: 16 (over y, core).
Axes of the slice: x: 4, y: 8, z: 12, core: 2. Of those that a mesh axis runs over, the one named last changes fastest.
Arguments:
- normed: bfloat16 [98304, 4096], P(('grp', 'intra')), may hold values from -6 to 6
- cotangent: bfloat16 [98304, 1024], P(('grp', 'intra')), may hold values from -0.01953125 to 0.01953125
- norm_gain: float32 [4096], replicated, may hold values from 0.25 to 4
- weights: bfloat16 [4096, 1024], P('intra'), may hold values from -6 to 6
- row_state: float32 [48, 16, 4, 16], P('grp', 'intra'), may hold values from 0.05 to 20
- col_state: float32 [8, 128], replicated, may hold values from 0.3 to 10
- owner_table: int32 [128, 1], replicated, may hold values from 0 to 47; in each aligned block of 128 rows (0 to 127, 128 to 255, ...) at most 4 rows name the same one
Outputs:
- new_weights: bfloat16 [4096, 1024], P('intra')
- row_moments: float32 [48, 16, 4, 16], P('grp', 'intra')
- col_moments: float32 [8, 128], replicated
The draws below stay inside these ranges and needn't reach their ends.
Inputs may be any that keep to these rules, and one draw needn't show every extreme that they name: `owner_table`: each group owns at most 4 units, some group exactly 4, and every group owns at least one.
All inputs are finite; a program needn't handle non-finite values.
Results may differ from the reference program's by a relative error of at most 0.013.
Values may be sent and summed in bfloat16 or wider, within the bound.
No kernel may reach another device: no remote copies, remote signals or barrier semaphores. Data moves between devices by JAX's collectives and lax.ppermute only.
A program may use at most 32 MiB of HBM per device.

```python
import math
import jax
import jax.numpy as jnp
import numpy as np
from jax import lax

D = 4096
HD = 128
NT = 8
TOK_DEV = 128
TOKENS = 98304
UR = 16
NB = 16
NU = 128
CAP = 4
N_GRP = 48
N_INTRA = 16


def shard_levels(rng, extent, cuts, least, high):
    factor_of = 1.0
    for position, shards_of in cuts:
        draws = jax.random.uniform(jax.random.fold_in(jax.random.fold_in(rng, 6), position), (shards_of,), jnp.float32, least / len(cuts), high / len(cuts))
        factor_of = factor_of * jnp.repeat(jnp.exp(draws), extent[position] // shards_of).reshape((-1,) + (1,) * (len(extent) - 1 - position))
    return factor_of


def shared_out(own_key, own, number, rows, count, top, most, slope):
    sequence = jax.random.permutation(own_key, count)
    crowded, usual = portions_of(count, rows * top, most, slope, True), portions_of(count, rows * top, most, slope, False)
    places = jnp.arange(count)

    def named(sizes, rotation):
        used = int((sizes > 0).sum())
        fixed = max(1, used // 4)
        moved = fixed + (places - fixed + rotation * (used - fixed)) % max(1, count - fixed)
        return jnp.zeros((count,), jnp.int32).at[sequence[jnp.where(places < fixed, places, moved)]].set(jnp.asarray(sizes, jnp.int32))

    sizes = jnp.where(number % 4 == 0, named(crowded, number // 4), named(usual, number - number // 4 - 1))
    mixed = jax.random.permutation(jax.random.fold_in(own, 3), count)
    donor, sink = mixed[0:count // 2 * 2:2], mixed[1:count // 2 * 2:2]
    room = jnp.minimum(sizes[donor] - 1, most - sizes[sink]) // 2
    room = jnp.where((donor == sequence[0]) | (sink == sequence[0]) | (sizes[sink] == 0), 0, jnp.maximum(room, 0))
    moved = jax.random.randint(jax.random.fold_in(own, 4), (count // 2,), 0, 1 << 20) % (room + 1)
    sizes = sizes.at[donor].add(-moved).at[sink].add(moved)
    items = jnp.searchsorted(jnp.cumsum(sizes), jnp.arange(rows * top), side="right").astype(jnp.int32)
    grid = items.reshape(top, rows).T
    grid = grid[jax.random.permutation(jax.random.fold_in(own, 1), rows)]
    rotation = jax.random.randint(jax.random.fold_in(own, 2), (rows, 1), 0, top)
    return jnp.take_along_axis(grid, (jnp.arange(top)[None, :] + rotation) % top, axis=1)


def portions_of(amount, total, most, lean, full):
    weights = [(1 << 20) // math.isqrt(rank ** lean) + 1 for rank in range(1, amount + 1)]
    largest = most if full else min(most, max(-(-total // amount), total * weights[0] // sum(weights)))
    least = 1 if total - largest >= amount - 1 else 0
    counts, rest = [largest] + [least] * (amount - 1), total - largest - least * (amount - 1)
    while rest > 0:
        candidates = [i for i in range(1, amount) if counts[i] < largest] or [i for i in range(1, amount) if counts[i] < most]
        whole, budget = sum([weights[i] for i in candidates]), rest
        for i in candidates:
            more = min(most - counts[i], max(1, budget * weights[i] // whole), rest)
            counts[i] = counts[i] + more
            rest = rest - more
    return np.array(counts)


def scatter_about(rng, extent, scale, reach, shards=(), kind=jnp.bfloat16):
    loudness = shard_levels(rng, extent, shards, -0.22, 0.18) if shards else 1.0
    values = jax.random.normal(rng, extent, jnp.float32) * scale * loudness
    return jnp.minimum(jnp.maximum(values, -reach), reach).astype(kind)


def setup_inputs(seed: int = 0) -> dict:
    arg_keys = jax.random.split(jax.random.key(seed), 8)
    normed = scatter_about(arg_keys[0], (TOKENS, D), 1.0, 6.0, ((0, 768),))
    cotangent = scatter_about(arg_keys[1], (TOKENS, NT * HD), TOKENS ** -0.5, 0.01953125, ((0, 768),))
    norm_gain = jnp.clip(jnp.exp(jax.random.uniform(arg_keys[2], (D,), jnp.float32, math.log(0.25), math.log(4.0))), 0.25, 4.0)
    weights = scatter_about(arg_keys[3], (D, NT * HD), 1.0, 6.0, ((0, 16),))
    row_state = jnp.clip(jnp.exp(math.log(20.0) - 5.9914645 * jax.random.uniform(arg_keys[4], (N_GRP, N_INTRA, CAP, UR), jnp.float32) ** shard_levels(arg_keys[4], (N_GRP, N_INTRA, CAP, UR), ((0, 48), (1, 16)), -0.2, 0.2)), 0.05, 20.0)
    col_state = jnp.clip(jnp.exp(jax.random.uniform(arg_keys[5], (NT, HD), jnp.float32, math.log(0.3), math.log(10.0))), 0.3, 10.0)
    owner_table_keys = jax.random.split(jax.random.fold_in(arg_keys[6], 1), NU // NU)
    owner_table_turns = jax.random.permutation(jax.random.fold_in(arg_keys[6], 3), NU // NU)
    owner_table = jax.vmap(lambda own, number: shared_out(jax.random.fold_in(arg_keys[6], 2), own, number, NU, N_GRP, 1, CAP, 2))(owner_table_keys, owner_table_turns).reshape((NU, 1))
    return dict(normed=normed, cotangent=cotangent, norm_gain=norm_gain, weights=weights, row_state=row_state, col_state=col_state, owner_table=owner_table)


decay_rate = 0.8
step_size = 0.5
epsilon = 1e-06

def slots_of(owner_flat):
    onehot = (owner_flat[:, None] == jnp.arange(N_GRP, dtype=jnp.int32)[None, :]).astype(jnp.int32)
    before = jnp.cumsum(onehot, axis=0) - onehot
    return lax.optimization_barrier(jnp.sum(before * onehot, axis=1)).astype(jnp.int32)

def reference(normed, cotangent, norm_gain, weights, row_state, col_state, owner_table):
    scaled = (normed * norm_gain[None, :]).astype(jnp.bfloat16)
    width = NT * HD
    acts = scaled.reshape(N_GRP, N_INTRA, TOK_DEV, D)
    grads = cotangent.reshape(N_GRP, N_INTRA, TOK_DEV, width)

    def member(total, pair):
        left, right = pair
        term = jnp.dot(left.T, right, preferred_element_type=jnp.float32).astype(jnp.bfloat16)
        term = lax.optimization_barrier(term)
        return (total + term.astype(jnp.float32), None)

    def group(total, pair):
        inner, _ = lax.scan(member, jnp.zeros((D, width), jnp.float32), pair)
        return (total + inner, None)
    grad, _ = lax.scan(group, jnp.zeros((D, width), jnp.float32), (acts, grads))
    cube_grad = grad.reshape(D, NT, HD)
    squares = cube_grad * cube_grad
    row_mean = lax.optimization_barrier(jnp.mean(squares, axis=2)) + epsilon
    col_mean = lax.optimization_barrier(jnp.mean(squares, axis=0)) + epsilon
    owner_flat = owner_table[:, 0].astype(jnp.int32)
    slot = slots_of(owner_flat)
    prev_units = row_state[owner_flat, :, slot, :]
    prev_rows = prev_units.reshape(NT, NB, N_INTRA, UR).transpose(0, 2, 1, 3).reshape(NT, D).T
    row_new = decay_rate * prev_rows + (1.0 - decay_rate) * row_mean
    row_avg = lax.optimization_barrier(jnp.mean(row_new, axis=0))
    col_new = decay_rate * col_state + (1.0 - decay_rate) * col_mean
    variance = row_new[:, :, None] * col_new[None, :, :] / row_avg[None, :, None]
    updated = weights.reshape(D, NT, HD).astype(jnp.float32) - step_size * cube_grad / jnp.sqrt(variance)
    new_weights = updated.reshape(D, width).astype(jnp.bfloat16)
    row_units = row_new.T.reshape(NT, N_INTRA, NB, UR).transpose(0, 2, 1, 3).reshape(NU, N_INTRA, UR)
    row_moments = jnp.zeros((N_GRP, N_INTRA, CAP, UR), jnp.float32).at[owner_flat, :, slot, :].set(row_units)
    return (new_weights, row_moments, col_new)
```

```python
import jax
import jax.numpy as jnp
from jax import lax
from jax.sharding import PartitionSpec as P

decay_rate = 0.8
step_size = 0.5
epsilon = 1e-06

N_X = 4
CORES = 2


def on_device(normed, cotangent, norm_gain, weights, row_state, col_state, owner_table):
    bf16, f32 = jnp.bfloat16, jnp.float32
    groups = lax.axis_size("grp")
    intra = lax.axis_size("intra")
    n_y = intra // CORES
    n_z = groups // N_X
    tokens, d_model = normed.shape
    tensors, head = col_state.shape
    width = tensors * head
    capacity, unit_rows = row_state.shape[2:]
    slab = weights.shape[0]
    blocks = slab // unit_rows
    units = tensors * blocks
    pair = CORES * slab

    same_core = [[y * CORES + c for y in range(n_y)] for c in range(CORES)]
    x_groups = [[z * N_X + x for x in range(N_X)] for z in range(n_z)]
    z_groups = [[z * N_X + x for z in range(n_z)] for x in range(N_X)]

    def shift(a, k):
        pairs = [
            (y * CORES + c, ((y + k) % n_y) * CORES + c) for y in range(n_y) for c in range(CORES)
        ]
        return lax.ppermute(a, "intra", pairs)

    me = lax.axis_index("intra")
    my_y, my_core = me // CORES, me % CORES
    my_group = lax.axis_index("grp")

    scaled = (normed * norm_gain[None, :]).astype(bf16)
    parts = scaled.reshape(tokens, n_y, pair).transpose(1, 0, 2)
    acts = lax.all_to_all(parts, "intra", 0, 0, axis_index_groups=same_core, tiled=True)
    chunks = {0: cotangent}
    up, down = cotangent, cotangent
    for k in range(1, n_y // 2 + 1):
        down = shift(down, -1)
        chunks[k] = down
        if k < n_y // 2:
            up = shift(up, 1)
            chunks[n_y - k] = up
    cots = jnp.concatenate([chunks[k] for k in range(n_y)], axis=0)
    acts = lax.dynamic_slice_in_dim(jnp.concatenate([acts, acts], axis=0), my_y, n_y, 0)
    partial = lax.dot_general(
        acts.reshape(n_y * tokens, pair), cots, (((0,), (0,)), ((), ())), preferred_element_type=f32
    )

    keep = lax.dynamic_slice_in_dim(partial, my_core * slab, slab, 0)
    give = lax.dynamic_slice_in_dim(partial, (1 - my_core) * slab, slab, 0).astype(bf16)
    swap = [(i, i ^ 1) for i in range(intra)]
    own = keep + lax.ppermute(give, "intra", swap).astype(f32)

    def to_units(a):
        return (
            a.reshape(blocks, unit_rows, tensors, head)
            .transpose(2, 0, 1, 3)
            .reshape(units, unit_rows, head)
        )

    per_x = units // N_X
    per_z = -(-per_x // n_z)
    sent = to_units(own.astype(bf16)).reshape(N_X, per_x * unit_rows, head)
    got = lax.all_to_all(sent, "grp", 0, 0, axis_index_groups=x_groups, tiled=True)
    summed = jnp.sum(got.astype(f32), axis=0).astype(bf16)
    summed = jnp.pad(summed, ((0, (per_z * n_z - per_x) * unit_rows), (0, 0)))
    got = lax.all_to_all(
        summed.reshape(n_z, per_z * unit_rows, head),
        "grp", 0, 0, axis_index_groups=z_groups, tiled=True,
    )
    chunk = jnp.sum(got.astype(f32), axis=0).astype(bf16)

    flat_state = row_state.reshape(1, capacity * unit_rows)
    high = flat_state.astype(bf16)
    low = (flat_state - high.astype(f32)).astype(bf16)
    state_row = jnp.concatenate([high, low], axis=1)
    state_width = state_row.shape[1]
    state_row = jnp.pad(state_row, ((0, unit_rows - 1), (0, head - state_width)))
    chunk = jnp.concatenate([chunk, state_row], axis=0)
    got = lax.all_to_all(
        jnp.broadcast_to(chunk[None], (n_z,) + chunk.shape),
        "grp", 0, 0, axis_index_groups=z_groups, tiled=True,
    )
    grads = got[:, : per_z * unit_rows].reshape(-1, head)[: per_x * unit_rows]
    states = got[:, per_z * unit_rows]
    pad = -n_z % unit_rows
    packed = jnp.concatenate([grads, jnp.pad(states, ((0, pad), (0, 0)))], axis=0)
    got = lax.all_to_all(
        jnp.broadcast_to(packed[None], (N_X,) + packed.shape),
        "grp", 0, 0, axis_index_groups=x_groups, tiled=True,
    )
    grad_units = got[:, : per_x * unit_rows].reshape(units, unit_rows, head).astype(f32)
    states = got[:, per_x * unit_rows : per_x * unit_rows + n_z]
    states = states.transpose(1, 0, 2).reshape(groups, head)
    half = capacity * unit_rows
    state_high = states[:, :half].reshape(groups * capacity, unit_rows)
    state_low = states[:, half : 2 * half].reshape(groups * capacity, unit_rows)

    owner = owner_table[:, 0]
    onehot = (owner[:, None] == jnp.arange(groups, dtype=jnp.int32)[None, :]).astype(jnp.int32)
    before = jnp.cumsum(onehot, axis=0) - onehot
    slot = jnp.sum(before * onehot, axis=1)
    place = owner * capacity + slot
    pick = (place[:, None] == jnp.arange(groups * capacity, dtype=jnp.int32)[None, :]).astype(bf16)
    prev = jnp.dot(pick, state_high, preferred_element_type=f32) + jnp.dot(
        pick, state_low, preferred_element_type=f32
    )

    squares = grad_units * grad_units
    row_mean = jnp.mean(squares, axis=2) + epsilon
    row_new = decay_rate * prev + (1.0 - decay_rate) * row_mean
    col_part = jnp.sum(squares.reshape(tensors, blocks * unit_rows, head), axis=1)
    row_part = jnp.sum(row_new.reshape(tensors, blocks * unit_rows), axis=1)
    stats = jnp.concatenate(
        [col_part, jnp.broadcast_to(row_part[:, None], (tensors, head))], axis=0
    )
    stats = lax.all_to_all(
        jnp.broadcast_to(stats[None], (intra,) + stats.shape), "intra", 0, 0, tiled=True
    )
    total = jnp.sum(stats, axis=0)
    col_total, row_total = total[:tensors], total[tensors:]
    col_new = decay_rate * col_state + (1.0 - decay_rate) * (col_total / d_model + epsilon)
    row_avg = row_total / d_model
    col_factor = col_new / row_avg
    variance = row_new.reshape(tensors, blocks * unit_rows, 1) * col_factor[:, None, :]
    weight_units = to_units(weights).reshape(tensors, blocks * unit_rows, head)
    updated = weight_units.astype(f32) - step_size * grad_units.reshape(
        tensors, blocks * unit_rows, head
    ) / jnp.sqrt(variance)
    new_weights = (
        updated.astype(bf16).transpose(1, 0, 2).reshape(slab, width)
    )

    mine = (
        place[None, :] == my_group * capacity + jnp.arange(capacity, dtype=jnp.int32)[:, None]
    )
    filled = jnp.any(mine, axis=1)
    own_mean = jnp.dot(mine.astype(f32), row_mean, precision=lax.Precision.HIGHEST)
    row_moments = jnp.where(
        filled[:, None], decay_rate * row_state[0, 0] + (1.0 - decay_rate) * own_mean, 0.0
    )
    return (new_weights, row_moments[None, None], col_new)


def solution(mesh):
    placed = (
        P(("grp", "intra"), None),
        P(("grp", "intra"), None),
        P(),
        P("intra", None),
        P("grp", "intra", None, None),
        P(),
        P(),
    )
    return jax.shard_map(
        on_device,
        mesh=mesh,
        in_specs=placed,
        out_specs=(P("intra", None), P("grp", "intra", None, None), P()),
        check_vma=False,
    )
```

```python
import functools

import jax
import jax.numpy as jnp
from jax import lax
from jax.experimental import pallas as pl
from jax.experimental.pallas import tpu as pltpu
from jax.sharding import PartitionSpec as P


decay_rate = 0.8
step_size = 0.5
epsilon = 1e-06

N_X = 4
CORES = 2


def arrange_kernel(slab, x_ref, gain_ref, mine_ref, theirs_ref):
    me = lax.axis_index("intra")
    my_y, my_core = me // CORES, me % CORES
    half = x_ref.shape[1] // (CORES * slab)
    n_y = 2 * half // CORES
    ahead = [n_y] + [2 * k + h for k in range(n_y // 2 - 1, 0, -1) for h in (0, 1)] + [1]
    behind = [n_y + 1] + [2 * k + h for k in range(n_y // 2 + 1, n_y) for h in (1, 0)] + [0]
    for out, up, down in ((theirs_ref, behind, ahead), (mine_ref, ahead, behind)):
        for u in range(half):
            piece = lax.rem(jnp.where(my_core == 0, up[u], down[u]) + 2 * my_y, 2 * half)
            column = pl.multiple_of(piece * slab, slab)
            block = x_ref[:, pl.ds(column, slab)].astype(jnp.float32)
            scaled = block * gain_ref[:, pl.ds(column, slab)]
            out[:, u * slab : (u + 1) * slab] = scaled.astype(out.dtype)


def arrange(x, gain, slab):
    tokens, d_model = x.shape
    half = jax.ShapeDtypeStruct((tokens, d_model // CORES), x.dtype)
    vmem = pl.BlockSpec(memory_space=pltpu.VMEM)
    return pl.pallas_call(
        functools.partial(arrange_kernel, slab),
        out_shape=(half, half),
        in_specs=[vmem, vmem],
        out_specs=(vmem, vmem),
        cost_estimate=pl.CostEstimate(
            flops=tokens * d_model, bytes_accessed=4 * tokens * d_model, transcendentals=0
        ),
        compiler_params=pltpu.CompilerParams(vmem_limit_bytes=12 << 20),
        name="arrange",
    )(x, gain)


def products_kernel(slab, begin, after, x_ref, xg_ref, c_ref, cg_ref, *outs):
    dims = (((0,), (0,)), ((), ()))
    for u, out in enumerate(outs[after:], begin):
        cols = slice(u * slab, (u + 1) * slab)
        total = lax.dot_general(
            x_ref[:, cols], c_ref[...], dims, preferred_element_type=jnp.float32
        ) + lax.dot_general(
            xg_ref[:, cols], cg_ref[...], dims, preferred_element_type=jnp.float32
        )
        out[...] = total.astype(out.dtype)


def products(mine, got, cot, cot_got, slab, begin, end, *after):
    tokens, _ = mine.shape
    width = cot.shape[1]
    count = end - begin
    vmem = pl.BlockSpec(memory_space=pltpu.VMEM)
    return pl.pallas_call(
        functools.partial(products_kernel, slab, begin, len(after)),
        out_shape=tuple(jax.ShapeDtypeStruct((slab, width), cot.dtype) for _ in range(count)),
        in_specs=[vmem] * 4 + [pl.BlockSpec(memory_space=pl.ANY)] * len(after),
        out_specs=tuple([vmem] * count),
        cost_estimate=pl.CostEstimate(
            flops=4 * tokens * count * slab * width,
            bytes_accessed=4 * count * slab * width,
            transcendentals=0,
        ),
        compiler_params=pltpu.CompilerParams(vmem_limit_bytes=16 << 20),
        name="products",
    )(mine, got, cot, cot_got, *after)


def finish_kernel(a_ref, b_ref, out_ref):
    head = out_ref.shape[2]
    slab = a_ref.shape[0]
    for t in range(a_ref.shape[1] // head):
        cols = slice(t * head, (t + 1) * head)
        total = a_ref[:, cols].astype(jnp.float32) + b_ref[:, cols].astype(jnp.float32)
        x, row = divmod(t * slab, out_ref.shape[1])
        out_ref[x, row : row + slab, :] = total.astype(out_ref.dtype)


def finish(a, b, head):
    vmem = pl.BlockSpec(memory_space=pltpu.VMEM)
    return pl.pallas_call(
        finish_kernel,
        out_shape=jax.ShapeDtypeStruct((N_X, a.size // (N_X * head), head), a.dtype),
        in_specs=[vmem, vmem],
        out_specs=vmem,
        cost_estimate=pl.CostEstimate(
            flops=a.size, bytes_accessed=6 * a.size, transcendentals=0
        ),
        compiler_params=pltpu.CompilerParams(vmem_limit_bytes=8 << 20),
        name="finish",
    )(a, b)


def on_device(normed, cotangent, norm_gain, weights, row_state, col_state, owner_table):
    bf16, f32 = jnp.bfloat16, jnp.float32
    groups = lax.axis_size("grp")
    intra = lax.axis_size("intra")
    n_y = intra // CORES
    n_z = groups // N_X
    _, d_model = normed.shape
    tensors, head = col_state.shape
    width = tensors * head
    capacity, unit_rows = row_state.shape[2:]
    slab = weights.shape[0]
    blocks = slab // unit_rows
    units = tensors * blocks

    x_groups = [[z * N_X + x for x in range(N_X)] for z in range(n_z)]
    z_groups = [[z * N_X + x for z in range(n_z)] for x in range(N_X)]

    my_group = lax.axis_index("grp")

    swap = [(i, i ^ 1) for i in range(intra)]
    cot_got = lax.ppermute(cotangent, "intra", swap)
    mine, theirs = arrange(normed, norm_gain[None, :], slab)
    got = lax.ppermute(theirs, "intra", swap)
    inputs = (mine, got, cotangent, cot_got, slab)
    parts = products(*inputs, 0, 1)
    parts = parts + products(*inputs, 1, mine.shape[1] // slab, parts[0])

    ring = [
        (y * CORES + c, ((y + 1 - 2 * c) % n_y) * CORES + c) for y in range(n_y) for c in range(CORES)
    ]

    def add(*terms):
        return sum(t.astype(f32) for t in terms)

    def hop(a):
        return lax.ppermute(a, "intra", ring)

    first, second = parts[0], parts[2]
    for k in range(1, len(parts) - 2, 2):
        first = add(hop(first), parts[k]).astype(bf16)
        if k > 1:
            second = add(hop(second), parts[k + 1]).astype(bf16)
    last = hop(first)
    give = add(hop(second), parts[-1]).astype(bf16)
    own = finish(last, lax.ppermute(give, "intra", swap), head)

    def to_units(a):
        return (
            a.reshape(blocks, unit_rows, tensors, head)
            .transpose(2, 0, 1, 3)
            .reshape(units, unit_rows, head)
        )

    per_x = units // N_X
    per_z = -(-per_x // n_z)
    got = lax.all_to_all(own, "grp", 0, 0, axis_index_groups=x_groups, tiled=True)
    summed = jnp.sum(got.astype(f32), axis=0).astype(bf16)
    summed = jnp.pad(summed, ((0, (per_z * n_z - per_x) * unit_rows), (0, 0)))
    got = lax.all_to_all(
        summed.reshape(n_z, per_z * unit_rows, head),
        "grp", 0, 0, axis_index_groups=z_groups, tiled=True,
    )
    chunk = jnp.sum(got.astype(f32), axis=0).astype(bf16)

    flat_state = row_state.reshape(1, capacity * unit_rows)
    high = flat_state.astype(bf16)
    low = (flat_state - high.astype(f32)).astype(bf16)
    state_row = jnp.concatenate([high, low], axis=1)
    state_width = state_row.shape[1]
    state_row = jnp.pad(state_row, ((0, unit_rows - 1), (0, head - state_width)))
    chunk = jnp.concatenate([chunk, state_row], axis=0)
    got = lax.all_to_all(
        jnp.broadcast_to(chunk[None], (n_z,) + chunk.shape),
        "grp", 0, 0, axis_index_groups=z_groups, tiled=True,
    )
    grads = got[:, : per_z * unit_rows].reshape(-1, head)[: per_x * unit_rows]
    states = got[:, per_z * unit_rows]
    pad = -n_z % unit_rows
    packed = jnp.concatenate([grads, jnp.pad(states, ((0, pad), (0, 0)))], axis=0)
    got = lax.all_to_all(
        jnp.broadcast_to(packed[None], (N_X,) + packed.shape),
        "grp", 0, 0, axis_index_groups=x_groups, tiled=True,
    )
    grad_units = got[:, : per_x * unit_rows].reshape(units, unit_rows, head).astype(f32)
    states = got[:, per_x * unit_rows : per_x * unit_rows + n_z]
    states = states.transpose(1, 0, 2).reshape(groups, head)
    half = capacity * unit_rows
    state_high = states[:, :half].reshape(groups * capacity, unit_rows)
    state_low = states[:, half : 2 * half].reshape(groups * capacity, unit_rows)

    owner = owner_table[:, 0]
    onehot = (owner[:, None] == jnp.arange(groups, dtype=jnp.int32)[None, :]).astype(jnp.int32)
    before = jnp.cumsum(onehot, axis=0) - onehot
    slot = jnp.sum(before * onehot, axis=1)
    place = owner * capacity + slot
    pick = (place[:, None] == jnp.arange(groups * capacity, dtype=jnp.int32)[None, :]).astype(bf16)
    prev = jnp.dot(pick, state_high, preferred_element_type=f32) + jnp.dot(
        pick, state_low, preferred_element_type=f32
    )

    squares = grad_units * grad_units
    row_mean = jnp.mean(squares, axis=2) + epsilon
    row_new = decay_rate * prev + (1.0 - decay_rate) * row_mean
    col_part = jnp.sum(squares.reshape(tensors, blocks * unit_rows, head), axis=1)
    row_part = jnp.sum(row_new.reshape(tensors, blocks * unit_rows), axis=1)
    stats = jnp.concatenate(
        [col_part, jnp.broadcast_to(row_part[:, None], (tensors, head))], axis=0
    )
    stats = lax.all_to_all(
        jnp.broadcast_to(stats[None], (intra,) + stats.shape), "intra", 0, 0, tiled=True
    )
    total = jnp.sum(stats, axis=0)
    col_total, row_total = total[:tensors], total[tensors:]
    col_new = decay_rate * col_state + (1.0 - decay_rate) * (col_total / d_model + epsilon)
    row_avg = row_total / d_model
    col_factor = col_new / row_avg
    variance = row_new.reshape(tensors, blocks * unit_rows, 1) * col_factor[:, None, :]
    weight_units = to_units(weights).reshape(tensors, blocks * unit_rows, head)
    updated = weight_units.astype(f32) - step_size * grad_units.reshape(
        tensors, blocks * unit_rows, head
    ) / jnp.sqrt(variance)
    new_weights = (
        updated.astype(bf16).transpose(1, 0, 2).reshape(slab, width)
    )

    mine = (
        place[None, :] == my_group * capacity + jnp.arange(capacity, dtype=jnp.int32)[:, None]
    )
    filled = jnp.any(mine, axis=1)
    own_mean = jnp.dot(mine.astype(f32), row_mean, precision=lax.Precision.HIGHEST)
    row_moments = jnp.where(
        filled[:, None], decay_rate * row_state[0, 0] + (1.0 - decay_rate) * own_mean, 0.0
    )
    return (new_weights, row_moments[None, None], col_new)


def solution(mesh):
    placed = (
        P(("grp", "intra"), None),
        P(("grp", "intra"), None),
        P(),
        P("intra", None),
        P("grp", "intra", None, None),
        P(),
        P(),
    )
    return jax.shard_map(
        on_device,
        mesh=mesh,
        in_specs=placed,
        out_specs=(P("intra", None), P("grp", "intra", None, None), P()),
        check_vma=False,
    )
```

```python
import functools

import jax
import jax.numpy as jnp
from jax import lax
from jax.experimental import pallas as pl
from jax.experimental.pallas import tpu as pltpu
from jax.sharding import PartitionSpec as P


decay_rate = 0.8
step_size = 0.5
epsilon = 1e-06

N_X = 4
CORES = 2


def arrange_kernel(slab, x_ref, gain_ref, mine_ref, theirs_ref):
    me = lax.axis_index("intra")
    my_y, my_core = me // CORES, me % CORES
    half = x_ref.shape[1] // (CORES * slab)
    n_y = 2 * half // CORES
    ahead = [n_y] + [2 * k + h for k in range(n_y // 2 - 1, 0, -1) for h in (0, 1)] + [1]
    behind = [n_y + 1] + [2 * k + h for k in range(n_y // 2 + 1, n_y) for h in (1, 0)] + [0]
    for out, up, down in ((theirs_ref, behind, ahead), (mine_ref, ahead, behind)):
        for u in range(half):
            piece = lax.rem(jnp.where(my_core == 0, up[u], down[u]) + 2 * my_y, 2 * half)
            column = pl.multiple_of(piece * slab, slab)
            block = x_ref[:, pl.ds(column, slab)].astype(jnp.float32)
            scaled = block * gain_ref[:, pl.ds(column, slab)]
            out[:, u * slab : (u + 1) * slab] = scaled.astype(out.dtype)


def arrange(x, gain, slab):
    tokens, d_model = x.shape
    half = jax.ShapeDtypeStruct((tokens, d_model // CORES), x.dtype)
    vmem = pl.BlockSpec(memory_space=pltpu.VMEM)
    return pl.pallas_call(
        functools.partial(arrange_kernel, slab),
        out_shape=(half, half),
        in_specs=[vmem, vmem],
        out_specs=(vmem, vmem),
        cost_estimate=pl.CostEstimate(
            flops=tokens * d_model, bytes_accessed=4 * tokens * d_model, transcendentals=0
        ),
        compiler_params=pltpu.CompilerParams(vmem_limit_bytes=12 << 20),
        name="arrange",
    )(x, gain)


def products_kernel(slab, begin, after, x_ref, xg_ref, c_ref, cg_ref, *outs):
    dims = (((0,), (0,)), ((), ()))
    for u, out in enumerate(outs[after:], begin):
        cols = slice(u * slab, (u + 1) * slab)
        total = lax.dot_general(
            x_ref[:, cols], c_ref[...], dims, preferred_element_type=jnp.float32
        ) + lax.dot_general(
            xg_ref[:, cols], cg_ref[...], dims, preferred_element_type=jnp.float32
        )
        out[...] = total.astype(out.dtype)


def products(mine, got, cot, cot_got, slab, begin, end, *after):
    tokens, _ = mine.shape
    width = cot.shape[1]
    count = end - begin
    vmem = pl.BlockSpec(memory_space=pltpu.VMEM)
    return pl.pallas_call(
        functools.partial(products_kernel, slab, begin, len(after)),
        out_shape=tuple(jax.ShapeDtypeStruct((slab, width), cot.dtype) for _ in range(count)),
        in_specs=[vmem] * 4 + [pl.BlockSpec(memory_space=pl.ANY)] * len(after),
        out_specs=tuple([vmem] * count),
        cost_estimate=pl.CostEstimate(
            flops=4 * tokens * count * slab * width,
            bytes_accessed=4 * count * slab * width,
            transcendentals=0,
        ),
        compiler_params=pltpu.CompilerParams(vmem_limit_bytes=16 << 20),
        name="products",
    )(mine, got, cot, cot_got, *after)


def finish_kernel(a_ref, b_ref, out_ref):
    head = out_ref.shape[2]
    slab = a_ref.shape[0]
    for t in range(a_ref.shape[1] // head):
        cols = slice(t * head, (t + 1) * head)
        total = a_ref[:, cols].astype(jnp.float32) + b_ref[:, cols].astype(jnp.float32)
        x, row = divmod(t * slab, out_ref.shape[1])
        out_ref[x, row : row + slab, :] = total.astype(out_ref.dtype)


def finish(a, b, head):
    vmem = pl.BlockSpec(memory_space=pltpu.VMEM)
    return pl.pallas_call(
        finish_kernel,
        out_shape=jax.ShapeDtypeStruct((N_X, a.size // (N_X * head), head), a.dtype),
        in_specs=[vmem, vmem],
        out_specs=vmem,
        cost_estimate=pl.CostEstimate(
            flops=a.size, bytes_accessed=6 * a.size, transcendentals=0
        ),
        compiler_params=pltpu.CompilerParams(vmem_limit_bytes=8 << 20),
        name="finish",
    )(a, b)


def small_kernel(body, out_shape, *operands):
    vmem = pl.BlockSpec(memory_space=pltpu.VMEM)
    size = sum(a.size for a in operands)
    return pl.pallas_call(
        body,
        out_shape=out_shape,
        in_specs=[vmem] * len(operands),
        out_specs=jax.tree.map(lambda _: vmem, out_shape),
        cost_estimate=pl.CostEstimate(flops=size, bytes_accessed=4 * size, transcendentals=0),
        compiler_params=pltpu.CompilerParams(vmem_limit_bytes=8 << 20),
    )(*operands)


def total_of(ref, rows=slice(None)):
    return sum(ref[j, rows, :].astype(jnp.float32) for j in range(ref.shape[0]))


def sum_x_kernel(got_ref, out_ref):
    rows = out_ref.shape[1]
    for j in range(out_ref.shape[0]):
        begin = min(j * rows, got_ref.shape[1])
        end = min(begin + rows, got_ref.shape[1])
        if end > begin:
            out_ref[j, : end - begin, :] = total_of(got_ref, slice(begin, end)).astype(out_ref.dtype)
        if end - begin < rows:
            out_ref[j, end - begin :, :] = jnp.zeros(
                (rows - end + begin, out_ref.shape[2]), out_ref.dtype
            )


def sum_z_kernel(got_ref, extra_ref, out_ref):
    rows = got_ref.shape[1]
    total = total_of(got_ref).astype(out_ref.dtype)
    for j in range(out_ref.shape[0]):
        out_ref[j, :rows, :] = total
        out_ref[j, rows:, :] = extra_ref[...]


def pack_kernel(rows, got_ref, out_ref):
    count = got_ref.shape[0]
    full = out_ref.shape[1] - (count + (-count) % 16)
    for x in range(out_ref.shape[0]):
        for j in range(count):
            begin = min(j * rows, full)
            end = min(begin + rows, full)
            if end > begin:
                out_ref[x, begin:end, :] = got_ref[j, : end - begin, :]
    tail = jnp.concatenate(
        [got_ref[j, rows : rows + 1, :].astype(jnp.float32) for j in range(count)]
        + [jnp.zeros(((-count) % 16, got_ref.shape[2]), jnp.float32)],
        axis=0,
    ).astype(out_ref.dtype)
    for x in range(out_ref.shape[0]):
        out_ref[x, full:, :] = tail


def on_device(normed, cotangent, norm_gain, weights, row_state, col_state, owner_table):
    bf16, f32 = jnp.bfloat16, jnp.float32
    groups = lax.axis_size("grp")
    intra = lax.axis_size("intra")
    n_y = intra // CORES
    n_z = groups // N_X
    _, d_model = normed.shape
    tensors, head = col_state.shape
    width = tensors * head
    capacity, unit_rows = row_state.shape[2:]
    slab = weights.shape[0]
    blocks = slab // unit_rows
    units = tensors * blocks

    x_groups = [[z * N_X + x for x in range(N_X)] for z in range(n_z)]
    z_groups = [[z * N_X + x for z in range(n_z)] for x in range(N_X)]

    my_group = lax.axis_index("grp")

    swap = [(i, i ^ 1) for i in range(intra)]
    cot_got = lax.ppermute(cotangent, "intra", swap)
    mine, theirs = arrange(normed, norm_gain[None, :], slab)
    got = lax.ppermute(theirs, "intra", swap)
    inputs = (mine, got, cotangent, cot_got, slab)
    parts = products(*inputs, 0, 1)
    parts = parts + products(*inputs, 1, mine.shape[1] // slab, parts[0])

    ring = [
        (y * CORES + c, ((y + 1 - 2 * c) % n_y) * CORES + c) for y in range(n_y) for c in range(CORES)
    ]

    def add(*terms):
        return sum(t.astype(f32) for t in terms)

    def hop(a):
        return lax.ppermute(a, "intra", ring)

    first, second = parts[0], parts[2]
    for k in range(1, len(parts) - 2, 2):
        first = add(hop(first), parts[k]).astype(bf16)
        if k > 1:
            second = add(hop(second), parts[k + 1]).astype(bf16)
    last = hop(first)
    give = add(hop(second), parts[-1]).astype(bf16)
    other = lax.ppermute(give, "intra", swap)
    own = finish(last, other, head)

    def to_units(a):
        return (
            a.reshape(blocks, unit_rows, tensors, head)
            .transpose(2, 0, 1, 3)
            .reshape(units, unit_rows, head)
        )

    per_x = units // N_X
    per_z = -(-per_x // n_z)
    got = lax.all_to_all(own, "grp", 0, 0, axis_index_groups=x_groups, tiled=True)
    sent = jax.ShapeDtypeStruct((n_z, per_z * unit_rows, head), bf16)
    sent = small_kernel(sum_x_kernel, sent, got)
    got = lax.all_to_all(sent, "grp", 0, 0, axis_index_groups=z_groups, tiled=True)

    flat_state = row_state.reshape(1, capacity * unit_rows)
    high = flat_state.astype(bf16)
    low = (flat_state - high.astype(f32)).astype(bf16)
    state_row = jnp.concatenate([high, low], axis=1)
    state_width = state_row.shape[1]
    state_row = jnp.pad(state_row, ((0, unit_rows - 1), (0, head - state_width)))
    sent = jax.ShapeDtypeStruct((n_z, got.shape[1] + unit_rows, head), bf16)
    sent = small_kernel(sum_z_kernel, sent, got, state_row)
    got = lax.all_to_all(sent, "grp", 0, 0, axis_index_groups=z_groups, tiled=True)
    sent = jax.ShapeDtypeStruct((N_X, per_x * unit_rows + n_z + -n_z % unit_rows, head), bf16)
    body = functools.partial(pack_kernel, per_z * unit_rows)
    sent = small_kernel(body, sent, got)
    got = lax.all_to_all(sent, "grp", 0, 0, axis_index_groups=x_groups, tiled=True)
    grad_units = got[:, : per_x * unit_rows].reshape(units, unit_rows, head).astype(f32)
    states = got[:, per_x * unit_rows : per_x * unit_rows + n_z]
    states = states.transpose(1, 0, 2).reshape(groups, head)
    half = capacity * unit_rows
    state_high = states[:, :half].reshape(groups * capacity, unit_rows)
    state_low = states[:, half : 2 * half].reshape(groups * capacity, unit_rows)

    owner = owner_table[:, 0]
    onehot = (owner[:, None] == jnp.arange(groups, dtype=jnp.int32)[None, :]).astype(jnp.int32)
    before = jnp.cumsum(onehot, axis=0) - onehot
    slot = jnp.sum(before * onehot, axis=1)
    place = owner * capacity + slot
    pick = (place[:, None] == jnp.arange(groups * capacity, dtype=jnp.int32)[None, :]).astype(bf16)
    prev = jnp.dot(pick, state_high, preferred_element_type=f32) + jnp.dot(
        pick, state_low, preferred_element_type=f32
    )

    squares = grad_units * grad_units
    row_mean = jnp.mean(squares, axis=2) + epsilon
    row_new = decay_rate * prev + (1.0 - decay_rate) * row_mean
    col_part = jnp.sum(squares.reshape(tensors, blocks * unit_rows, head), axis=1)
    row_part = jnp.sum(row_new.reshape(tensors, blocks * unit_rows), axis=1)
    stats = jnp.concatenate(
        [col_part, jnp.broadcast_to(row_part[:, None], (tensors, head))], axis=0
    )
    stats = lax.all_to_all(
        jnp.broadcast_to(stats[None], (intra,) + stats.shape), "intra", 0, 0, tiled=True
    )
    total = jnp.sum(stats, axis=0)
    col_total, row_total = total[:tensors], total[tensors:]
    col_new = decay_rate * col_state + (1.0 - decay_rate) * (col_total / d_model + epsilon)
    row_avg = row_total / d_model
    col_factor = col_new / row_avg
    variance = row_new.reshape(tensors, blocks * unit_rows, 1) * col_factor[:, None, :]
    weight_units = to_units(weights).reshape(tensors, blocks * unit_rows, head)
    updated = weight_units.astype(f32) - step_size * grad_units.reshape(
        tensors, blocks * unit_rows, head
    ) / jnp.sqrt(variance)
    new_weights = (
        updated.astype(bf16).transpose(1, 0, 2).reshape(slab, width)
    )

    mine = (
        place[None, :] == my_group * capacity + jnp.arange(capacity, dtype=jnp.int32)[:, None]
    )
    filled = jnp.any(mine, axis=1)
    own_mean = jnp.dot(mine.astype(f32), row_mean, precision=lax.Precision.HIGHEST)
    row_moments = jnp.where(
        filled[:, None], decay_rate * row_state[0, 0] + (1.0 - decay_rate) * own_mean, 0.0
    )
    return (new_weights, row_moments[None, None], col_new)


def solution(mesh):
    placed = (
        P(("grp", "intra"), None),
        P(("grp", "intra"), None),
        P(),
        P("intra", None),
        P("grp", "intra", None, None),
        P(),
        P(),
    )
    return jax.shard_map(
        on_device,
        mesh=mesh,
        in_specs=placed,
        out_specs=(P("intra", None), P("grp", "intra", None, None), P()),
        check_vma=False,
    )
```

```python
import functools

import jax
import jax.numpy as jnp
from jax import lax
from jax.experimental import pallas as pl
from jax.experimental.pallas import tpu as pltpu
from jax.sharding import PartitionSpec as P


decay_rate = 0.8
step_size = 0.5
epsilon = 1e-06

N_X = 4
CORES = 2


def arrange_kernel(slab, x_ref, gain_ref, mine_ref, theirs_ref):
    me = lax.axis_index("intra")
    my_y, my_core = me // CORES, me % CORES
    half = x_ref.shape[1] // (CORES * slab)
    n_y = 2 * half // CORES
    ahead = [n_y] + [2 * k + h for k in range(n_y // 2 - 1, 0, -1) for h in (0, 1)] + [1]
    behind = [n_y + 1] + [2 * k + h for k in range(n_y // 2 + 1, n_y) for h in (1, 0)] + [0]
    for out, up, down in ((theirs_ref, behind, ahead), (mine_ref, ahead, behind)):
        for u in range(half):
            piece = lax.rem(jnp.where(my_core == 0, up[u], down[u]) + 2 * my_y, 2 * half)
            column = pl.multiple_of(piece * slab, slab)
            block = x_ref[:, pl.ds(column, slab)].astype(jnp.float32)
            scaled = block * gain_ref[:, pl.ds(column, slab)]
            out[:, u * slab : (u + 1) * slab] = scaled.astype(out.dtype)


def arrange(x, gain, slab):
    tokens, d_model = x.shape
    half = jax.ShapeDtypeStruct((tokens, d_model // CORES), x.dtype)
    vmem = pl.BlockSpec(memory_space=pltpu.VMEM)
    return pl.pallas_call(
        functools.partial(arrange_kernel, slab),
        out_shape=(half, half),
        in_specs=[vmem, vmem],
        out_specs=(vmem, vmem),
        cost_estimate=pl.CostEstimate(
            flops=tokens * d_model, bytes_accessed=4 * tokens * d_model, transcendentals=0
        ),
        compiler_params=pltpu.CompilerParams(vmem_limit_bytes=12 << 20),
        name="arrange",
    )(x, gain)


def products_kernel(slab, begin, after, x_ref, xg_ref, c_ref, cg_ref, *outs):
    dims = (((0,), (0,)), ((), ()))
    for u, out in enumerate(outs[after:], begin):
        cols = slice(u * slab, (u + 1) * slab)
        total = lax.dot_general(
            x_ref[:, cols], c_ref[...], dims, preferred_element_type=jnp.float32
        ) + lax.dot_general(
            xg_ref[:, cols], cg_ref[...], dims, preferred_element_type=jnp.float32
        )
        out[...] = total.astype(out.dtype)


def products(mine, got, cot, cot_got, slab, begin, end, *after):
    tokens, _ = mine.shape
    width = cot.shape[1]
    count = end - begin
    vmem = pl.BlockSpec(memory_space=pltpu.VMEM)
    return pl.pallas_call(
        functools.partial(products_kernel, slab, begin, len(after)),
        out_shape=tuple(jax.ShapeDtypeStruct((slab, width), cot.dtype) for _ in range(count)),
        in_specs=[vmem] * 4 + [pl.BlockSpec(memory_space=pl.ANY)] * len(after),
        out_specs=tuple([vmem] * count),
        cost_estimate=pl.CostEstimate(
            flops=4 * tokens * count * slab * width,
            bytes_accessed=4 * count * slab * width,
            transcendentals=0,
        ),
        compiler_params=pltpu.CompilerParams(vmem_limit_bytes=16 << 20),
        name="products",
    )(mine, got, cot, cot_got, *after)


def finish_kernel(a_ref, b_ref, out_ref):
    head = out_ref.shape[2]
    slab = a_ref.shape[0]
    for t in range(a_ref.shape[1] // head):
        cols = slice(t * head, (t + 1) * head)
        total = a_ref[:, cols].astype(jnp.float32) + b_ref[:, cols].astype(jnp.float32)
        x, row = divmod(t * slab, out_ref.shape[1])
        out_ref[x, row : row + slab, :] = total.astype(out_ref.dtype)


def finish(a, b, head):
    vmem = pl.BlockSpec(memory_space=pltpu.VMEM)
    return pl.pallas_call(
        finish_kernel,
        out_shape=jax.ShapeDtypeStruct((N_X, a.size // (N_X * head), head), a.dtype),
        in_specs=[vmem, vmem],
        out_specs=vmem,
        cost_estimate=pl.CostEstimate(
            flops=a.size, bytes_accessed=6 * a.size, transcendentals=0
        ),
        compiler_params=pltpu.CompilerParams(vmem_limit_bytes=8 << 20),
        name="finish",
    )(a, b)


def small_kernel(body, out_shape, *operands):
    vmem = pl.BlockSpec(memory_space=pltpu.VMEM)
    size = sum(a.size for a in operands)
    return pl.pallas_call(
        body,
        out_shape=out_shape,
        in_specs=[vmem] * len(operands),
        out_specs=jax.tree.map(lambda _: vmem, out_shape),
        cost_estimate=pl.CostEstimate(flops=size, bytes_accessed=4 * size, transcendentals=0),
        compiler_params=pltpu.CompilerParams(vmem_limit_bytes=8 << 20),
    )(*operands)


def total_of(ref, rows=slice(None)):
    return sum(ref[j, rows, :].astype(jnp.float32) for j in range(ref.shape[0]))


def sum_x_kernel(got_ref, out_ref):
    rows = out_ref.shape[1]
    for j in range(out_ref.shape[0]):
        begin = min(j * rows, got_ref.shape[1])
        end = min(begin + rows, got_ref.shape[1])
        if end > begin:
            out_ref[j, : end - begin, :] = total_of(got_ref, slice(begin, end)).astype(out_ref.dtype)
        if end - begin < rows:
            out_ref[j, end - begin :, :] = jnp.zeros(
                (rows - end + begin, out_ref.shape[2]), out_ref.dtype
            )


def sum_z_kernel(got_ref, extra_ref, out_ref):
    rows = got_ref.shape[1]
    total = total_of(got_ref).astype(out_ref.dtype)
    for j in range(out_ref.shape[0]):
        out_ref[j, :rows, :] = total
        out_ref[j, rows:, :] = extra_ref[...]


def pack_kernel(rows, got_ref, out_ref, stats_ref):
    count, _, head = got_ref.shape
    pad = -count % 16
    full = out_ref.shape[0] - count - pad
    cols = [jnp.zeros((1, head), jnp.float32)] * 2
    for j in range(count):
        begin = min(j * rows, full)
        end = min(begin + rows, full)
        if end > begin:
            out_ref[begin:end, :] = got_ref[j, : end - begin, :]
        for t in range(2):
            low, high = max(begin, t * full // 2), min(end, (t + 1) * full // 2)
            if high > low:
                part = got_ref[j, low - begin : high - begin, :].astype(jnp.float32)
                cols[t] = cols[t] + jnp.sum(part * part, axis=0, keepdims=True)
    extra = [got_ref[j, rows : rows + 16, :].astype(jnp.float32) for j in range(count)]
    tail = [e[:1] for e in extra] + [jnp.zeros((pad, head), jnp.float32)]
    tail = jnp.concatenate(tail, axis=0).astype(out_ref.dtype)
    out_ref[full:, :] = tail
    sums = sum(e[1:2] for e in extra)
    stats = cols + [sums, jnp.zeros((stats_ref.shape[1] - 3, head), jnp.float32)]
    stats = jnp.concatenate(stats, axis=0)
    for j in range(stats_ref.shape[0]):
        stats_ref[j] = stats


def rows_kernel(pick_ref, lane_ref, *refs):
    *got, out_ref, mean_ref = refs
    my_x = lax.axis_index("grp") % N_X
    head = out_ref.shape[1]
    full = out_ref.shape[0] // N_X
    slab = full // 2
    states = jnp.concatenate([ref[full:, :] for ref in got], axis=0)
    for k, ref in enumerate(got):
        for t in range(2):
            begin = ((my_x + k) % N_X) * full + t * slab
            where = pl.ds(pl.multiple_of(begin, slab), slab)
            grad = ref[t * slab : (t + 1) * slab, :].astype(jnp.float32)
            state = jnp.dot(pick_ref[where, :], states, preferred_element_type=jnp.float32)
            prev = jnp.sum(state * lane_ref[where, :].astype(jnp.float32), axis=1, keepdims=True)
            mean = jnp.sum(grad * grad, axis=1, keepdims=True) / head + epsilon
            mean_ref[where, :] = jnp.broadcast_to(mean, (slab, mean_ref.shape[1]))
            out_ref[where, :] = grad * lax.rsqrt(decay_rate * prev + (1.0 - decay_rate) * mean)


def update_kernel(stats_ref, grad_ref, weight_ref, state_ref, out_ref, col_ref):
    tensors, head = state_ref.shape
    slab = weight_ref.shape[0]
    d_model = slab * stats_ref.shape[0] // N_X
    plane = stats_ref.shape[0] // N_X
    sums = jnp.sum(stats_ref[:, 2, :], axis=0, keepdims=True)
    for t in range(tensors):
        x = t // 2
        col = jnp.sum(stats_ref[x * plane : (x + 1) * plane, t % 2, :], axis=0, keepdims=True)
        col = col / d_model + epsilon
        col_new = decay_rate * state_ref[t : t + 1, :] + (1.0 - decay_rate) * col
        col_ref[t : t + 1, :] = col_new
        prev = (sums[:, t : t + 1] + sums[:, tensors + t : tensors + t + 1]) / d_model
        average = decay_rate * prev + (1.0 - decay_rate) * jnp.mean(col, axis=1, keepdims=True)
        factor = step_size * lax.rsqrt(col_new / average)
        cols = slice(t * head, (t + 1) * head)
        change = grad_ref[t * slab : (t + 1) * slab, :] * factor
        out_ref[:, cols] = (weight_ref[:, cols].astype(jnp.float32) - change).astype(out_ref.dtype)


def on_device(normed, cotangent, norm_gain, weights, row_state, col_state, owner_table):
    bf16, f32 = jnp.bfloat16, jnp.float32
    groups = lax.axis_size("grp")
    intra = lax.axis_size("intra")
    n_y = intra // CORES
    n_z = groups // N_X
    tensors, head = col_state.shape
    capacity, unit_rows = row_state.shape[2:]
    slab = weights.shape[0]
    blocks = slab // unit_rows
    units = tensors * blocks

    x_groups = [[z * N_X + x for x in range(N_X)] for z in range(n_z)]
    z_groups = [[z * N_X + x for z in range(n_z)] for x in range(N_X)]

    my_group = lax.axis_index("grp")

    swap = [(i, i ^ 1) for i in range(intra)]
    cot_got = lax.ppermute(cotangent, "intra", swap)
    mine, theirs = arrange(normed, norm_gain[None, :], slab)
    got = lax.ppermute(theirs, "intra", swap)
    inputs = (mine, got, cotangent, cot_got, slab)
    parts = products(*inputs, 0, 1)
    parts = parts + products(*inputs, 1, mine.shape[1] // slab, parts[0])

    ring = [
        (y * CORES + c, ((y + 1 - 2 * c) % n_y) * CORES + c) for y in range(n_y) for c in range(CORES)
    ]

    def add(*terms):
        return sum(t.astype(f32) for t in terms)

    def hop(a):
        return lax.ppermute(a, "intra", ring)

    first, second = parts[0], parts[2]
    for k in range(1, len(parts) - 2, 2):
        first = add(hop(first), parts[k]).astype(bf16)
        if k > 1:
            second = add(hop(second), parts[k + 1]).astype(bf16)
    last = hop(first)
    give = add(hop(second), parts[-1]).astype(bf16)
    other = lax.ppermute(give, "intra", swap)
    own = finish(last, other, head)

    per_x = units // N_X
    per_z = -(-per_x // n_z)
    got = lax.all_to_all(own, "grp", 0, 0, axis_index_groups=x_groups, tiled=True)
    sent = jax.ShapeDtypeStruct((n_z, per_z * unit_rows, head), bf16)
    sent = small_kernel(sum_x_kernel, sent, got)
    got = lax.all_to_all(sent, "grp", 0, 0, axis_index_groups=z_groups, tiled=True)

    owner = owner_table[:, 0]
    onehot = (owner[:, None] == jnp.arange(groups, dtype=jnp.int32)[None, :]).astype(jnp.int32)
    before = jnp.cumsum(onehot, axis=0) - onehot
    slot = jnp.sum(before * onehot, axis=1)
    place = owner * capacity + slot
    mine = (
        place[None, :] == my_group * capacity + jnp.arange(capacity, dtype=jnp.int32)[:, None]
    )
    filled = jnp.any(mine, axis=1)

    def two_parts(a):
        high = a.astype(bf16)
        return jnp.concatenate([high, (a - high.astype(f32)).astype(bf16)], axis=1)

    state_sum = jnp.where(filled, jnp.sum(row_state[0, 0], axis=1), 0.0)
    of_tensor = jnp.any(mine.reshape(capacity, tensors, blocks), axis=2)
    sums = jnp.sum(jnp.where(of_tensor, state_sum[:, None], 0.0), axis=0)
    half = capacity * unit_rows
    rows = [two_parts(row_state.reshape(1, half)), two_parts(sums[None, :])]
    rows = [jnp.pad(r, ((0, 0), (0, head - r.shape[1]))) for r in rows]
    extra = jnp.concatenate(rows + [jnp.zeros((unit_rows - 2, head), bf16)], axis=0)
    sent = jax.ShapeDtypeStruct((n_z, got.shape[1] + unit_rows, head), bf16)
    sent = small_kernel(sum_z_kernel, sent, got, extra)
    got = lax.all_to_all(sent, "grp", 0, 0, axis_index_groups=z_groups, tiled=True)
    full = per_x * unit_rows
    state_rows = n_z + -n_z % unit_rows
    shapes = (
        jax.ShapeDtypeStruct((full + state_rows, head), bf16),
        jax.ShapeDtypeStruct((N_X * intra, 8, head), f32),
    )
    body = functools.partial(pack_kernel, per_z * unit_rows)
    sent, stats = small_kernel(body, shapes, got)
    plane = N_X * intra
    planes = [list(range(z * plane, (z + 1) * plane)) for z in range(n_z)]
    stats = lax.all_to_all(
        stats, ("grp", "intra"), 0, 0, axis_index_groups=planes, tiled=True
    )
    fetched = [sent]
    for k in range(1, N_X):
        pairs = [
            (z * N_X + (x + k) % N_X, z * N_X + x) for z in range(n_z) for x in range(N_X)
        ]
        fetched.append(lax.ppermute(sent, "grp", pairs))

    seat = ((owner - my_group) % N_X) * state_rows + owner // N_X
    pick = seat[:, None, None] == jnp.arange(N_X * state_rows, dtype=jnp.int32)
    pick = jnp.broadcast_to(pick, (units, unit_rows, N_X * state_rows)).astype(bf16)
    lane = slot[:, None, None] * unit_rows + jnp.arange(unit_rows, dtype=jnp.int32)[None, :, None]
    lane = (lane == jnp.arange(head, dtype=jnp.int32) % half).astype(bf16)
    count = units * unit_rows
    shapes = (
        jax.ShapeDtypeStruct((count, head), f32),
        jax.ShapeDtypeStruct((count, 8), f32),
    )
    scaled, row_mean = small_kernel(
        rows_kernel, shapes, pick.reshape(count, -1), lane.reshape(count, head), *fetched
    )
    shapes = (
        jax.ShapeDtypeStruct(weights.shape, weights.dtype),
        jax.ShapeDtypeStruct(col_state.shape, f32),
    )
    new_weights, col_new = small_kernel(update_kernel, shapes, stats, scaled, weights, col_state)
    row_mean = row_mean[:, 0].reshape(units, unit_rows)
    own_mean = jnp.dot(mine.astype(f32), row_mean, precision=lax.Precision.HIGHEST)
    row_moments = jnp.where(
        filled[:, None], decay_rate * row_state[0, 0] + (1.0 - decay_rate) * own_mean, 0.0
    )
    return (new_weights, row_moments[None, None], col_new)


def solution(mesh):
    placed = (
        P(("grp", "intra"), None),
        P(("grp", "intra"), None),
        P(),
        P("intra", None),
        P("grp", "intra", None, None),
        P(),
        P(),
    )
    return jax.shard_map(
        on_device,
        mesh=mesh,
        in_specs=placed,
        out_specs=(P("intra", None), P("grp", "intra", None, None), P()),
        check_vma=False,
    )
```

```python
import functools

import jax
import jax.numpy as jnp
from jax import lax
from jax.experimental import pallas as pl
from jax.experimental.pallas import tpu as pltpu
from jax.sharding import PartitionSpec as P


decay_rate = 0.8
step_size = 0.5
epsilon = 1e-06

N_X = 4
CORES = 2


def arrange_kernel(slab, x_ref, gain_ref, mine_ref, theirs_ref):
    me = lax.axis_index("intra")
    my_y, my_core = me // CORES, me % CORES
    half = x_ref.shape[1] // (CORES * slab)
    n_y = 2 * half // CORES
    ahead = [n_y] + [2 * k + h for k in range(n_y // 2 - 1, 0, -1) for h in (0, 1)] + [1]
    behind = [n_y + 1] + [2 * k + h for k in range(n_y // 2 + 1, n_y) for h in (1, 0)] + [0]
    for out, up, down in ((theirs_ref, behind, ahead), (mine_ref, ahead, behind)):
        for u in range(half):
            piece = lax.rem(jnp.where(my_core == 0, up[u], down[u]) + 2 * my_y, 2 * half)
            column = pl.multiple_of(piece * slab, slab)
            block = x_ref[:, pl.ds(column, slab)].astype(jnp.float32)
            scaled = block * gain_ref[:, pl.ds(column, slab)]
            out[:, u * slab : (u + 1) * slab] = scaled.astype(out.dtype)


def arrange(x, gain, slab):
    tokens, d_model = x.shape
    half = jax.ShapeDtypeStruct((tokens, d_model // CORES), x.dtype)
    vmem = pl.BlockSpec(memory_space=pltpu.VMEM)
    return pl.pallas_call(
        functools.partial(arrange_kernel, slab),
        out_shape=(half, half),
        in_specs=[vmem, vmem],
        out_specs=(vmem, vmem),
        cost_estimate=pl.CostEstimate(
            flops=tokens * d_model, bytes_accessed=4 * tokens * d_model, transcendentals=0
        ),
        compiler_params=pltpu.CompilerParams(vmem_limit_bytes=12 << 20),
        name="arrange",
    )(x, gain)


def products_kernel(slab, begin, after, x_ref, xg_ref, c_ref, cg_ref, *outs):
    dims = (((0,), (0,)), ((), ()))
    for u, out in enumerate(outs[after:], begin):
        cols = slice(u * slab, (u + 1) * slab)
        total = lax.dot_general(
            x_ref[:, cols], c_ref[...], dims, preferred_element_type=jnp.float32
        ) + lax.dot_general(
            xg_ref[:, cols], cg_ref[...], dims, preferred_element_type=jnp.float32
        )
        out[...] = total.astype(out.dtype)


def products(mine, got, cot, cot_got, slab, begin, end, *after):
    tokens, _ = mine.shape
    width = cot.shape[1]
    count = end - begin
    vmem = pl.BlockSpec(memory_space=pltpu.VMEM)
    return pl.pallas_call(
        functools.partial(products_kernel, slab, begin, len(after)),
        out_shape=tuple(jax.ShapeDtypeStruct((slab, width), cot.dtype) for _ in range(count)),
        in_specs=[vmem] * 4 + [pl.BlockSpec(memory_space=pl.ANY)] * len(after),
        out_specs=tuple([vmem] * count),
        cost_estimate=pl.CostEstimate(
            flops=4 * tokens * count * slab * width,
            bytes_accessed=4 * count * slab * width,
            transcendentals=0,
        ),
        compiler_params=pltpu.CompilerParams(vmem_limit_bytes=16 << 20),
        name="products",
    )(mine, got, cot, cot_got, *after)


def finish_kernel(a_ref, b_ref, out_ref):
    head = out_ref.shape[2]
    slab = a_ref.shape[0]
    for t in range(a_ref.shape[1] // head):
        cols = slice(t * head, (t + 1) * head)
        total = a_ref[:, cols].astype(jnp.float32) + b_ref[:, cols].astype(jnp.float32)
        x, row = divmod(t * slab, out_ref.shape[1])
        out_ref[x, row : row + slab, :] = total.astype(out_ref.dtype)


def finish(a, b, head):
    vmem = pl.BlockSpec(memory_space=pltpu.VMEM)
    return pl.pallas_call(
        finish_kernel,
        out_shape=jax.ShapeDtypeStruct((N_X, a.size // (N_X * head), head), a.dtype),
        in_specs=[vmem, vmem],
        out_specs=vmem,
        cost_estimate=pl.CostEstimate(
            flops=a.size, bytes_accessed=6 * a.size, transcendentals=0
        ),
        compiler_params=pltpu.CompilerParams(vmem_limit_bytes=8 << 20),
        name="finish",
    )(a, b)


def small_kernel(body, out_shape, *operands, scalars=0, scratch=()):
    vmem = pl.BlockSpec(memory_space=pltpu.VMEM)
    smem = pl.BlockSpec(memory_space=pltpu.SMEM)
    size = sum(a.size for a in operands)
    return pl.pallas_call(
        body,
        out_shape=out_shape,
        in_specs=[smem] * scalars + [vmem] * (len(operands) - scalars),
        out_specs=jax.tree.map(lambda _: vmem, out_shape),
        scratch_shapes=scratch,
        cost_estimate=pl.CostEstimate(flops=size, bytes_accessed=4 * size, transcendentals=0),
        compiler_params=pltpu.CompilerParams(vmem_limit_bytes=8 << 20),
    )(*operands)


def total_of(ref, rows=slice(None)):
    return sum(ref[j, rows, :].astype(jnp.float32) for j in range(ref.shape[0]))


def sum_x_kernel(got_ref, out_ref):
    rows = out_ref.shape[1]
    for j in range(out_ref.shape[0]):
        begin = min(j * rows, got_ref.shape[1])
        end = min(begin + rows, got_ref.shape[1])
        if end > begin:
            out_ref[j, : end - begin, :] = total_of(got_ref, slice(begin, end)).astype(out_ref.dtype)
        if end - begin < rows:
            out_ref[j, end - begin :, :] = jnp.zeros(
                (rows - end + begin, out_ref.shape[2]), out_ref.dtype
            )


def sum_z_kernel(got_ref, extra_ref, out_ref):
    rows = got_ref.shape[1]
    total = total_of(got_ref).astype(out_ref.dtype)
    for j in range(out_ref.shape[0]):
        out_ref[j, :rows, :] = total
        out_ref[j, rows:, :] = extra_ref[...]


def pack_kernel(rows, got_ref, out_ref, stats_ref):
    count, _, head = got_ref.shape
    pad = -count % 16
    full = out_ref.shape[0] - count - pad
    cols = [jnp.zeros((1, head), jnp.float32)] * 2
    for j in range(count):
        begin = min(j * rows, full)
        end = min(begin + rows, full)
        if end > begin:
            out_ref[begin:end, :] = got_ref[j, : end - begin, :]
        for t in range(2):
            low, high = max(begin, t * full // 2), min(end, (t + 1) * full // 2)
            if high > low:
                part = got_ref[j, low - begin : high - begin, :].astype(jnp.float32)
                cols[t] = cols[t] + jnp.sum(part * part, axis=0, keepdims=True)
    extra = [got_ref[j, rows : rows + 16, :].astype(jnp.float32) for j in range(count)]
    tail = [e[:1] for e in extra] + [jnp.zeros((pad, head), jnp.float32)]
    tail = jnp.concatenate(tail, axis=0).astype(out_ref.dtype)
    out_ref[full:, :] = tail
    sums = sum(e[1:2] for e in extra)
    stats = cols + [sums, jnp.zeros((stats_ref.shape[1] - 3, head), jnp.float32)]
    stats = jnp.concatenate(stats, axis=0)
    for j in range(stats_ref.shape[0]):
        stats_ref[j] = stats


def rows_kernel(index_ref, state_ref, pick_ref, lane_ref, *refs):
    *got, out_ref, own_ref, mean_ref = refs
    my_x = lax.axis_index("grp") % N_X
    head = out_ref.shape[1]
    full = out_ref.shape[0] // N_X
    slab = full // 2
    states = jnp.concatenate([ref[full:, :] for ref in got], axis=0)
    for k, ref in enumerate(got):
        for t in range(2):
            begin = (my_x ^ k) * full + t * slab
            where = pl.ds(pl.multiple_of(begin, slab), slab)
            grad = ref[t * slab : (t + 1) * slab, :].astype(jnp.float32)
            state = jnp.dot(pick_ref[where, :], states, preferred_element_type=jnp.float32)
            prev = jnp.sum(state * lane_ref[where, :].astype(jnp.float32), axis=1, keepdims=True)
            mean = jnp.sum(grad * grad, axis=1, keepdims=True) / head + epsilon
            mean_ref[where, :] = jnp.broadcast_to(mean, (slab, head))
            out_ref[where, :] = grad * lax.rsqrt(decay_rate * prev + (1.0 - decay_rate) * mean)
    capacity, unit_rows = own_ref.shape
    shape = (unit_rows, unit_rows)
    eye = lax.broadcasted_iota(jnp.int32, shape, 0) == lax.broadcasted_iota(jnp.int32, shape, 1)
    for c in range(capacity):
        unit = jnp.maximum(index_ref[c], 0)
        column = mean_ref[pl.ds(pl.multiple_of(unit * unit_rows, unit_rows), unit_rows), :]
        mean = jnp.sum(jnp.where(eye, column[:, :unit_rows], 0.0), axis=0, keepdims=True)
        new = decay_rate * state_ref[c : c + 1, :] + (1.0 - decay_rate) * mean
        own_ref[c : c + 1, :] = jnp.where(index_ref[c] >= 0, new, 0.0)


def update_kernel(stats_ref, grad_ref, weight_ref, state_ref, out_ref, col_ref):
    tensors, head = state_ref.shape
    slab = weight_ref.shape[0]
    d_model = slab * stats_ref.shape[0] // N_X
    plane = stats_ref.shape[0] // N_X
    sums = jnp.sum(stats_ref[:, 2, :], axis=0, keepdims=True)
    for t in range(tensors):
        x = t // 2
        col = jnp.sum(stats_ref[x * plane : (x + 1) * plane, t % 2, :], axis=0, keepdims=True)
        col = col / d_model + epsilon
        col_new = decay_rate * state_ref[t : t + 1, :] + (1.0 - decay_rate) * col
        col_ref[t : t + 1, :] = col_new
        prev = (sums[:, t : t + 1] + sums[:, tensors + t : tensors + t + 1]) / d_model
        average = decay_rate * prev + (1.0 - decay_rate) * jnp.mean(col, axis=1, keepdims=True)
        factor = step_size * lax.rsqrt(col_new / average)
        cols = slice(t * head, (t + 1) * head)
        change = grad_ref[t * slab : (t + 1) * slab, :] * factor
        out_ref[:, cols] = (weight_ref[:, cols].astype(jnp.float32) - change).astype(out_ref.dtype)


def tables_kernel(owner_ref, state_ref, pick_ref, lane_ref, extra_ref, index_ref):
    f32, bf16 = jnp.float32, jnp.bfloat16
    me = lax.axis_index("grp")
    units = owner_ref.shape[0]
    capacity, unit_rows = state_ref.shape
    count, head = lane_ref.shape
    half = capacity * unit_rows
    tensors = units // unit_rows
    seats = pick_ref.shape[1]

    def at(shape, axis):
        return lax.broadcasted_iota(jnp.int32, shape, axis)

    owner = owner_ref[...]
    hot = (owner == at((units, head), 1)).astype(f32)
    earlier = (at((units, units), 1) < at((units, units), 0)).astype(bf16)
    before = jnp.dot(earlier, hot.astype(bf16), preferred_element_type=f32)
    slot = jnp.sum(before * hot, axis=1, keepdims=True).astype(jnp.int32)

    seat = ((owner ^ me) & (N_X - 1)) * (seats // N_X) + owner // N_X
    spread = ((at((count, units), 0) // unit_rows) == at((count, units), 1)).astype(bf16)
    hot = (seat == at((units, seats), 1)).astype(bf16)
    pick_ref[...] = jnp.dot(spread, hot, preferred_element_type=f32).astype(bf16)
    lanes = at((units, head), 1)
    hot = (slot == (lanes % half) // unit_rows).astype(bf16)
    match = (at((count, head), 0) % unit_rows) == (at((count, head), 1) % unit_rows)
    hot = jnp.dot(spread, hot, preferred_element_type=f32)
    lane_ref[...] = jnp.where(match, hot, 0.0).astype(bf16)

    state = state_ref[...]
    high = state.astype(bf16)
    low = (state - high.astype(f32)).astype(bf16)
    copies = (at((unit_rows, head), 0) == at((unit_rows, head), 1) % unit_rows).astype(bf16)
    high = jnp.dot(high, copies, preferred_element_type=f32)
    low = jnp.dot(low, copies, preferred_element_type=f32)
    lanes = at((capacity, head), 1)
    parts = jnp.where(lanes < half, high, low)
    mine = (lanes % half) // unit_rows == at((capacity, head), 0)
    state_row = jnp.sum(jnp.where(mine, parts, 0.0), axis=0, keepdims=True)
    number = at((units, 1), 0)
    sums = jnp.zeros((units, 1), f32)
    for c in range(capacity):
        here = (owner == me) & (slot == c)
        total = jnp.sum(state[c : c + 1, :], axis=1, keepdims=True)
        sums = sums + jnp.where(here, total, 0.0)
        index_ref[c] = jnp.max(jnp.where(here, number.astype(f32), -1.0)).astype(jnp.int32)
    lanes = at((units, head), 1)
    tensor = at((units, head), 0) // unit_rows
    here = (lanes % tensors == tensor) & (lanes < 2 * tensors)
    value = jnp.sum(jnp.where(here, sums, 0.0), axis=0, keepdims=True)
    high = value.astype(bf16).astype(f32)
    sum_row = jnp.where(at((1, head), 1) < tensors, high, value - high)
    rows = [state_row, sum_row, jnp.zeros((extra_ref.shape[0] - 2, head), f32)]
    extra_ref[...] = jnp.concatenate(rows, axis=0).astype(bf16)


def tables(owner_table, state, head, seats):
    capacity, unit_rows = state.shape
    count = owner_table.shape[0] * unit_rows
    vmem = pl.BlockSpec(memory_space=pltpu.VMEM)
    smem = pl.BlockSpec(memory_space=pltpu.SMEM)
    bf16 = jnp.bfloat16
    return pl.pallas_call(
        tables_kernel,
        out_shape=(
            jax.ShapeDtypeStruct((count, seats), bf16),
            jax.ShapeDtypeStruct((count, head), bf16),
            jax.ShapeDtypeStruct((unit_rows, head), bf16),
            jax.ShapeDtypeStruct((capacity,), jnp.int32),
        ),
        in_specs=[vmem, vmem],
        out_specs=(vmem, vmem, vmem, smem),
        cost_estimate=pl.CostEstimate(
            flops=count * head * 100, bytes_accessed=4 * count * head, transcendentals=0
        ),
        compiler_params=pltpu.CompilerParams(vmem_limit_bytes=8 << 20),
        name="tables",
    )(owner_table, state)


def on_device(normed, cotangent, norm_gain, weights, row_state, col_state, owner_table):
    bf16, f32 = jnp.bfloat16, jnp.float32
    groups = lax.axis_size("grp")
    intra = lax.axis_size("intra")
    n_y = intra // CORES
    n_z = groups // N_X
    tensors, head = col_state.shape
    capacity, unit_rows = row_state.shape[2:]
    slab = weights.shape[0]
    blocks = slab // unit_rows
    units = tensors * blocks

    x_groups = [[z * N_X + x for x in range(N_X)] for z in range(n_z)]
    z_groups = [[z * N_X + x for z in range(n_z)] for x in range(N_X)]


    swap = [(i, i ^ 1) for i in range(intra)]
    cot_got = lax.ppermute(cotangent, "intra", swap)
    mine, theirs = arrange(normed, norm_gain[None, :], slab)
    got = lax.ppermute(theirs, "intra", swap)
    inputs = (mine, got, cotangent, cot_got, slab)
    parts = products(*inputs, 0, 1)
    parts = parts + products(*inputs, 1, mine.shape[1] // slab, parts[0])

    ring = [
        (y * CORES + c, ((y + 1 - 2 * c) % n_y) * CORES + c) for y in range(n_y) for c in range(CORES)
    ]

    def add(*terms):
        return sum(t.astype(f32) for t in terms)

    def hop(a):
        return lax.ppermute(a, "intra", ring)

    first, second = parts[0], parts[2]
    for k in range(1, len(parts) - 2, 2):
        first = add(hop(first), parts[k]).astype(bf16)
        if k > 1:
            second = add(hop(second), parts[k + 1]).astype(bf16)
    last = hop(first)
    give = add(hop(second), parts[-1]).astype(bf16)
    other = lax.ppermute(give, "intra", swap)
    state_rows = n_z + -n_z % unit_rows
    pick, lane, extra, my_index = tables(owner_table, row_state[0, 0], head, N_X * state_rows)
    last, other, extra, pick, lane, my_index = lax.optimization_barrier(
        (last, other, extra, pick, lane, my_index)
    )
    own = finish(last, other, head)


    per_x = units // N_X
    per_z = -(-per_x // n_z)
    got = lax.all_to_all(own, "grp", 0, 0, axis_index_groups=x_groups, tiled=True)
    sent = jax.ShapeDtypeStruct((n_z, per_z * unit_rows, head), bf16)
    sent = small_kernel(sum_x_kernel, sent, got)
    got = lax.all_to_all(sent, "grp", 0, 0, axis_index_groups=z_groups, tiled=True)

    sent = jax.ShapeDtypeStruct((n_z, got.shape[1] + unit_rows, head), bf16)
    sent = small_kernel(sum_z_kernel, sent, got, extra)
    got = lax.all_to_all(sent, "grp", 0, 0, axis_index_groups=z_groups, tiled=True)
    full = per_x * unit_rows
    shapes = (
        jax.ShapeDtypeStruct((full + state_rows, head), bf16),
        jax.ShapeDtypeStruct((N_X * intra, 8, head), f32),
    )
    body = functools.partial(pack_kernel, per_z * unit_rows)
    sent, stats = small_kernel(body, shapes, got)
    plane = N_X * intra
    planes = [list(range(z * plane, (z + 1) * plane)) for z in range(n_z)]
    stats = lax.all_to_all(
        stats, ("grp", "intra"), 0, 0, axis_index_groups=planes, tiled=True
    )

    def trade(a, k):
        pairs = [(g, g ^ k) for g in range(groups)]
        return lax.ppermute(a, "grp", pairs)

    near, wrap = trade(sent, 1), trade(sent, N_X - 1)
    fetched = [sent, near, trade(near, N_X - 1), wrap]

    count = units * unit_rows
    shapes = (
        jax.ShapeDtypeStruct((count, head), f32),
        jax.ShapeDtypeStruct((capacity, unit_rows), f32),
    )
    scaled, row_moments = small_kernel(
        rows_kernel,
        shapes,
        my_index,
        row_state[0, 0],
        pick,
        lane,
        *fetched,
        scalars=1,
        scratch=[pltpu.VMEM((count, head), f32)],
    )
    shapes = (
        jax.ShapeDtypeStruct(weights.shape, weights.dtype),
        jax.ShapeDtypeStruct(col_state.shape, f32),
    )
    new_weights, col_new = small_kernel(update_kernel, shapes, stats, scaled, weights, col_state)
    return (new_weights, row_moments[None, None], col_new)


def solution(mesh):
    placed = (
        P(("grp", "intra"), None),
        P(("grp", "intra"), None),
        P(),
        P("intra", None),
        P("grp", "intra", None, None),
        P(),
        P(),
    )
    return jax.shard_map(
        on_device,
        mesh=mesh,
        in_specs=placed,
        out_specs=(P("intra", None), P("grp", "intra", None, None), P()),
        check_vma=False,
    )
```

```python
import functools

import jax
import jax.numpy as jnp
from jax import lax
from jax.experimental import pallas as pl
from jax.experimental.pallas import tpu as pltpu
from jax.sharding import PartitionSpec as P


decay_rate = 0.8
step_size = 0.5
epsilon = 1e-06

N_X = 4
CORES = 2


def arrange_kernel(slab, x_ref, gain_ref, mine_ref, theirs_ref):
    me = lax.axis_index("intra")
    my_y, my_core = me // CORES, me % CORES
    half = x_ref.shape[1] // (CORES * slab)
    n_y = 2 * half // CORES
    ahead = [n_y] + [2 * k + h for k in range(n_y // 2 - 1, 0, -1) for h in (0, 1)] + [1]
    behind = [n_y + 1] + [2 * k + h for k in range(n_y // 2 + 1, n_y) for h in (1, 0)] + [0]
    for out, up, down in ((theirs_ref, behind, ahead), (mine_ref, ahead, behind)):
        for u in range(half):
            piece = lax.rem(jnp.where(my_core == 0, up[u], down[u]) + 2 * my_y, 2 * half)
            column = pl.multiple_of(piece * slab, slab)
            block = x_ref[:, pl.ds(column, slab)].astype(jnp.float32)
            scaled = block * gain_ref[:, pl.ds(column, slab)]
            out[:, u * slab : (u + 1) * slab] = scaled.astype(out.dtype)


def arrange(x, gain, slab):
    tokens, d_model = x.shape
    half = jax.ShapeDtypeStruct((tokens, d_model // CORES), x.dtype)
    vmem = pl.BlockSpec(memory_space=pltpu.VMEM)
    return pl.pallas_call(
        functools.partial(arrange_kernel, slab),
        out_shape=(half, half),
        in_specs=[vmem, vmem],
        out_specs=(vmem, vmem),
        cost_estimate=pl.CostEstimate(
            flops=tokens * d_model, bytes_accessed=4 * tokens * d_model, transcendentals=0
        ),
        compiler_params=pltpu.CompilerParams(vmem_limit_bytes=12 << 20),
        name="arrange",
    )(x, gain)


def products_kernel(slab, begin, after, x_ref, xg_ref, c_ref, cg_ref, *outs):
    dims = (((0,), (0,)), ((), ()))
    outs = outs[after:]
    half = outs[0].shape[1]
    for u in range(begin, begin + len(outs) // 2):
        cols = slice(u * slab, (u + 1) * slab)
        total = lax.dot_general(
            x_ref[:, cols], c_ref[...], dims, preferred_element_type=jnp.float32
        ) + lax.dot_general(
            xg_ref[:, cols], cg_ref[...], dims, preferred_element_type=jnp.float32
        )
        for h in range(2):
            out = outs[2 * (u - begin) + h]
            out[...] = total[:, h * half : (h + 1) * half].astype(out.dtype)


def products(mine, got, cot, cot_got, slab, begin, end, *after):
    tokens, _ = mine.shape
    width = cot.shape[1]
    count = end - begin
    vmem = pl.BlockSpec(memory_space=pltpu.VMEM)
    return pl.pallas_call(
        functools.partial(products_kernel, slab, begin, len(after)),
        out_shape=tuple(
            jax.ShapeDtypeStruct((slab, width // 2), cot.dtype) for _ in range(2 * count)
        ),
        in_specs=[vmem] * 4 + [pl.BlockSpec(memory_space=pl.ANY)] * len(after),
        out_specs=tuple([vmem] * (2 * count)),
        cost_estimate=pl.CostEstimate(
            flops=4 * tokens * count * slab * width,
            bytes_accessed=4 * count * slab * width,
            transcendentals=0,
        ),
        compiler_params=pltpu.CompilerParams(vmem_limit_bytes=16 << 20),
        name="products",
    )(mine, got, cot, cot_got, *after)


def finish_kernel(*refs):
    *halves, out_ref = refs
    head = out_ref.shape[2]
    slab, width = halves[0].shape
    for t in range(2 * width // head):
        h, column = divmod(t * head, width)
        cols = slice(column, column + head)
        total = halves[h][:, cols].astype(jnp.float32) + halves[2 + h][:, cols].astype(jnp.float32)
        x, row = divmod(t * slab, out_ref.shape[1])
        out_ref[x, row : row + slab, :] = total.astype(out_ref.dtype)


def small_kernel(body, out_shape, *operands, scalars=0, scratch=()):
    vmem = pl.BlockSpec(memory_space=pltpu.VMEM)
    smem = pl.BlockSpec(memory_space=pltpu.SMEM)
    size = sum(a.size for a in operands)
    return pl.pallas_call(
        body,
        out_shape=out_shape,
        in_specs=[smem] * scalars + [vmem] * (len(operands) - scalars),
        out_specs=jax.tree.map(lambda _: vmem, out_shape),
        scratch_shapes=scratch,
        cost_estimate=pl.CostEstimate(flops=size, bytes_accessed=4 * size, transcendentals=0),
        compiler_params=pltpu.CompilerParams(vmem_limit_bytes=8 << 20),
    )(*operands)


def total_of(ref, rows=slice(None)):
    return sum(ref[j, rows, :].astype(jnp.float32) for j in range(ref.shape[0]))


def sum_x_kernel(got_ref, out_ref):
    rows = out_ref.shape[1]
    for j in range(out_ref.shape[0]):
        begin = min(j * rows, got_ref.shape[1])
        end = min(begin + rows, got_ref.shape[1])
        if end > begin:
            out_ref[j, : end - begin, :] = total_of(got_ref, slice(begin, end)).astype(out_ref.dtype)
        if end - begin < rows:
            out_ref[j, end - begin :, :] = jnp.zeros(
                (rows - end + begin, out_ref.shape[2]), out_ref.dtype
            )


def sum_z_kernel(got_ref, extra_ref, out_ref):
    rows = got_ref.shape[1]
    total = total_of(got_ref).astype(out_ref.dtype)
    for j in range(out_ref.shape[0]):
        out_ref[j, :rows, :] = total
        out_ref[j, rows:, :] = extra_ref[...]


def pack_kernel(rows, got_ref, out_ref, stats_ref):
    count, _, head = got_ref.shape
    pad = -count % 16
    full = out_ref.shape[0] - count - pad
    cols = [jnp.zeros((1, head), jnp.float32)] * 2
    for j in range(count):
        begin = min(j * rows, full)
        end = min(begin + rows, full)
        if end > begin:
            out_ref[begin:end, :] = got_ref[j, : end - begin, :]
        for t in range(2):
            low, high = max(begin, t * full // 2), min(end, (t + 1) * full // 2)
            if high > low:
                part = got_ref[j, low - begin : high - begin, :].astype(jnp.float32)
                cols[t] = cols[t] + jnp.sum(part * part, axis=0, keepdims=True)
    extra = [got_ref[j, rows : rows + 16, :].astype(jnp.float32) for j in range(count)]
    tail = [e[:1] for e in extra] + [jnp.zeros((pad, head), jnp.float32)]
    tail = jnp.concatenate(tail, axis=0).astype(out_ref.dtype)
    out_ref[full:, :] = tail
    sums = sum(e[1:2] for e in extra)
    stats = cols + [sums, jnp.zeros((stats_ref.shape[1] - 3, head), jnp.float32)]
    stats = jnp.concatenate(stats, axis=0)
    for j in range(stats_ref.shape[0]):
        stats_ref[j] = stats


def rows_kernel(index_ref, state_ref, pick_ref, lane_ref, *refs):
    *got, out_ref, own_ref, mean_ref = refs
    my_x = lax.axis_index("grp") % N_X
    head = out_ref.shape[1]
    full = out_ref.shape[0] // N_X
    slab = full // 2
    states = jnp.concatenate([ref[full:, :] for ref in got], axis=0)
    for k, ref in enumerate(got):
        for t in range(2):
            begin = (my_x ^ k) * full + t * slab
            where = pl.ds(pl.multiple_of(begin, slab), slab)
            grad = ref[t * slab : (t + 1) * slab, :].astype(jnp.float32)
            state = jnp.dot(pick_ref[where, :], states, preferred_element_type=jnp.float32)
            prev = jnp.sum(state * lane_ref[where, :].astype(jnp.float32), axis=1, keepdims=True)
            mean = jnp.sum(grad * grad, axis=1, keepdims=True) / head + epsilon
            mean_ref[where, :] = jnp.broadcast_to(mean, (slab, head))
            out_ref[where, :] = grad * lax.rsqrt(decay_rate * prev + (1.0 - decay_rate) * mean)
    capacity, unit_rows = own_ref.shape
    shape = (unit_rows, unit_rows)
    eye = lax.broadcasted_iota(jnp.int32, shape, 0) == lax.broadcasted_iota(jnp.int32, shape, 1)
    for c in range(capacity):
        unit = jnp.maximum(index_ref[c], 0)
        column = mean_ref[pl.ds(pl.multiple_of(unit * unit_rows, unit_rows), unit_rows), :]
        mean = jnp.sum(jnp.where(eye, column[:, :unit_rows], 0.0), axis=0, keepdims=True)
        new = decay_rate * state_ref[c : c + 1, :] + (1.0 - decay_rate) * mean
        own_ref[c : c + 1, :] = jnp.where(index_ref[c] >= 0, new, 0.0)


def update_kernel(stats_ref, grad_ref, weight_ref, state_ref, out_ref, col_ref):
    tensors, head = state_ref.shape
    slab = weight_ref.shape[0]
    d_model = slab * stats_ref.shape[0] // N_X
    plane = stats_ref.shape[0] // N_X
    sums = jnp.sum(stats_ref[:, 2, :], axis=0, keepdims=True)
    for t in range(tensors):
        x = t // 2
        col = jnp.sum(stats_ref[x * plane : (x + 1) * plane, t % 2, :], axis=0, keepdims=True)
        col = col / d_model + epsilon
        col_new = decay_rate * state_ref[t : t + 1, :] + (1.0 - decay_rate) * col
        col_ref[t : t + 1, :] = col_new
        prev = (sums[:, t : t + 1] + sums[:, tensors + t : tensors + t + 1]) / d_model
        average = decay_rate * prev + (1.0 - decay_rate) * jnp.mean(col, axis=1, keepdims=True)
        factor = step_size * lax.rsqrt(col_new / average)
        cols = slice(t * head, (t + 1) * head)
        change = grad_ref[t * slab : (t + 1) * slab, :] * factor
        out_ref[:, cols] = (weight_ref[:, cols].astype(jnp.float32) - change).astype(out_ref.dtype)


def tables_kernel(owner_ref, state_ref, pick_ref, lane_ref, extra_ref, index_ref):
    f32, bf16 = jnp.float32, jnp.bfloat16
    me = lax.axis_index("grp")
    units = owner_ref.shape[0]
    capacity, unit_rows = state_ref.shape
    count, head = lane_ref.shape
    half = capacity * unit_rows
    tensors = units // unit_rows
    seats = pick_ref.shape[1]

    def at(shape, axis):
        return lax.broadcasted_iota(jnp.int32, shape, axis)

    owner = owner_ref[...]
    hot = (owner == at((units, head), 1)).astype(f32)
    earlier = (at((units, units), 1) < at((units, units), 0)).astype(bf16)
    before = jnp.dot(earlier, hot.astype(bf16), preferred_element_type=f32)
    slot = jnp.sum(before * hot, axis=1, keepdims=True).astype(jnp.int32)

    seat = ((owner ^ me) & (N_X - 1)) * (seats // N_X) + owner // N_X
    spread = ((at((count, units), 0) // unit_rows) == at((count, units), 1)).astype(bf16)
    hot = (seat == at((units, seats), 1)).astype(bf16)
    pick_ref[...] = jnp.dot(spread, hot, preferred_element_type=f32).astype(bf16)
    lanes = at((units, head), 1)
    hot = (slot == (lanes % half) // unit_rows).astype(bf16)
    match = (at((count, head), 0) % unit_rows) == (at((count, head), 1) % unit_rows)
    hot = jnp.dot(spread, hot, preferred_element_type=f32)
    lane_ref[...] = jnp.where(match, hot, 0.0).astype(bf16)

    state = state_ref[...]
    high = state.astype(bf16)
    low = (state - high.astype(f32)).astype(bf16)
    copies = (at((unit_rows, head), 0) == at((unit_rows, head), 1) % unit_rows).astype(bf16)
    high = jnp.dot(high, copies, preferred_element_type=f32)
    low = jnp.dot(low, copies, preferred_element_type=f32)
    lanes = at((capacity, head), 1)
    parts = jnp.where(lanes < half, high, low)
    mine = (lanes % half) // unit_rows == at((capacity, head), 0)
    state_row = jnp.sum(jnp.where(mine, parts, 0.0), axis=0, keepdims=True)
    number = at((units, 1), 0)
    sums = jnp.zeros((units, 1), f32)
    for c in range(capacity):
        here = (owner == me) & (slot == c)
        total = jnp.sum(state[c : c + 1, :], axis=1, keepdims=True)
        sums = sums + jnp.where(here, total, 0.0)
        index_ref[c] = jnp.max(jnp.where(here, number.astype(f32), -1.0)).astype(jnp.int32)
    lanes = at((units, head), 1)
    tensor = at((units, head), 0) // unit_rows
    here = (lanes % tensors == tensor) & (lanes < 2 * tensors)
    value = jnp.sum(jnp.where(here, sums, 0.0), axis=0, keepdims=True)
    high = value.astype(bf16).astype(f32)
    sum_row = jnp.where(at((1, head), 1) < tensors, high, value - high)
    rows = [state_row, sum_row, jnp.zeros((extra_ref.shape[0] - 2, head), f32)]
    extra_ref[...] = jnp.concatenate(rows, axis=0).astype(bf16)


def tables(owner_table, state, head, seats):
    capacity, unit_rows = state.shape
    count = owner_table.shape[0] * unit_rows
    vmem = pl.BlockSpec(memory_space=pltpu.VMEM)
    smem = pl.BlockSpec(memory_space=pltpu.SMEM)
    bf16 = jnp.bfloat16
    return pl.pallas_call(
        tables_kernel,
        out_shape=(
            jax.ShapeDtypeStruct((count, seats), bf16),
            jax.ShapeDtypeStruct((count, head), bf16),
            jax.ShapeDtypeStruct((unit_rows, head), bf16),
            jax.ShapeDtypeStruct((capacity,), jnp.int32),
        ),
        in_specs=[vmem, vmem],
        out_specs=(vmem, vmem, vmem, smem),
        cost_estimate=pl.CostEstimate(
            flops=count * head * 100, bytes_accessed=4 * count * head, transcendentals=0
        ),
        compiler_params=pltpu.CompilerParams(vmem_limit_bytes=8 << 20),
        name="tables",
    )(owner_table, state)


def on_device(normed, cotangent, norm_gain, weights, row_state, col_state, owner_table):
    bf16, f32 = jnp.bfloat16, jnp.float32
    groups = lax.axis_size("grp")
    intra = lax.axis_size("intra")
    n_y = intra // CORES
    n_z = groups // N_X
    tensors, head = col_state.shape
    width = tensors * head
    capacity, unit_rows = row_state.shape[2:]
    slab = weights.shape[0]
    blocks = slab // unit_rows
    units = tensors * blocks

    x_groups = [[z * N_X + x for x in range(N_X)] for z in range(n_z)]
    z_groups = [[z * N_X + x for z in range(n_z)] for x in range(N_X)]


    swap = [(i, i ^ 1) for i in range(intra)]
    cot_got = lax.ppermute(cotangent, "intra", swap)
    mine, theirs = arrange(normed, norm_gain[None, :], slab)
    got = lax.ppermute(theirs, "intra", swap)
    inputs = (mine, got, cotangent, cot_got, slab)
    parts = products(*inputs, 0, 1)
    parts = parts + products(*inputs, 1, mine.shape[1] // slab, parts[0])

    ring = [
        (y * CORES + c, ((y + 1 - 2 * c) % n_y) * CORES + c) for y in range(n_y) for c in range(CORES)
    ]

    def add(*terms):
        return sum(t.astype(f32) for t in terms)

    def hop(a):
        return lax.ppermute(a, "intra", ring)

    parts = [parts[2 * k : 2 * k + 2] for k in range(len(parts) // 2)]
    first, second = list(parts[0]), list(parts[2])
    for k in range(1, len(parts) - 2, 2):
        for h in range(2):
            first[h] = add(hop(first[h]), parts[k][h]).astype(bf16)
            if k > 1:
                second[h] = add(hop(second[h]), parts[k + 1][h]).astype(bf16)
    last, other = [], []
    for h in range(2):
        last.append(hop(first[h]))
        give = add(hop(second[h]), parts[-1][h]).astype(bf16)
        other.append(lax.ppermute(give, "intra", swap))

    state_rows = n_z + -n_z % unit_rows
    pick, lane, extra, my_index = tables(owner_table, row_state[0, 0], head, N_X * state_rows)
    last, other, extra, pick, lane, my_index = lax.optimization_barrier(
        (last, other, extra, pick, lane, my_index)
    )
    own = jax.ShapeDtypeStruct((N_X, slab * width // (N_X * head), head), bf16)
    own = small_kernel(finish_kernel, own, *last, *other)


    per_x = units // N_X
    per_z = -(-per_x // n_z)
    got = lax.all_to_all(own, "grp", 0, 0, axis_index_groups=x_groups, tiled=True)
    sent = jax.ShapeDtypeStruct((n_z, per_z * unit_rows, head), bf16)
    sent = small_kernel(sum_x_kernel, sent, got)
    got = lax.all_to_all(sent, "grp", 0, 0, axis_index_groups=z_groups, tiled=True)

    sent = jax.ShapeDtypeStruct((n_z, got.shape[1] + unit_rows, head), bf16)
    sent = small_kernel(sum_z_kernel, sent, got, extra)
    got = lax.all_to_all(sent, "grp", 0, 0, axis_index_groups=z_groups, tiled=True)
    full = per_x * unit_rows
    shapes = (
        jax.ShapeDtypeStruct((full + state_rows, head), bf16),
        jax.ShapeDtypeStruct((N_X * intra, 8, head), f32),
    )
    body = functools.partial(pack_kernel, per_z * unit_rows)
    sent, stats = small_kernel(body, shapes, got)
    plane = N_X * intra
    planes = [list(range(z * plane, (z + 1) * plane)) for z in range(n_z)]
    stats = lax.all_to_all(
        stats, ("grp", "intra"), 0, 0, axis_index_groups=planes, tiled=True
    )

    def trade(a, k):
        pairs = [(g, g ^ k) for g in range(groups)]
        return lax.ppermute(a, "grp", pairs)

    near, wrap = trade(sent, 1), trade(sent, N_X - 1)
    fetched = [sent, near, trade(near, N_X - 1), wrap]

    count = units * unit_rows
    shapes = (
        jax.ShapeDtypeStruct((count, head), f32),
        jax.ShapeDtypeStruct((capacity, unit_rows), f32),
    )
    scaled, row_moments = small_kernel(
        rows_kernel,
        shapes,
        my_index,
        row_state[0, 0],
        pick,
        lane,
        *fetched,
        scalars=1,
        scratch=[pltpu.VMEM((count, head), f32)],
    )
    shapes = (
        jax.ShapeDtypeStruct(weights.shape, weights.dtype),
        jax.ShapeDtypeStruct(col_state.shape, f32),
    )
    new_weights, col_new = small_kernel(update_kernel, shapes, stats, scaled, weights, col_state)
    return (new_weights, row_moments[None, None], col_new)


def solution(mesh):
    placed = (
        P(("grp", "intra"), None),
        P(("grp", "intra"), None),
        P(),
        P("intra", None),
        P("grp", "intra", None, None),
        P(),
        P(),
    )
    return jax.shard_map(
        on_device,
        mesh=mesh,
        in_specs=placed,
        out_specs=(P("intra", None), P("grp", "intra", None, None), P()),
        check_vma=False,
    )
```

```python
import functools

import jax
import jax.numpy as jnp
from jax import lax
from jax.experimental import pallas as pl
from jax.experimental.pallas import tpu as pltpu
from jax.sharding import PartitionSpec as P


decay_rate = 0.8
step_size = 0.5
epsilon = 1e-06

N_X = 4
CORES = 2


def arrange_kernel(slab, x_ref, gain_ref, mine_ref, theirs_ref):
    me = lax.axis_index("intra")
    my_y, my_core = me // CORES, me % CORES
    half = x_ref.shape[1] // (CORES * slab)
    n_y = 2 * half // CORES
    ahead = [n_y] + [2 * k + h for k in range(n_y // 2 - 1, 0, -1) for h in (0, 1)] + [1]
    behind = [n_y + 1] + [2 * k + h for k in range(n_y // 2 + 1, n_y) for h in (1, 0)] + [0]
    for out, up, down in ((theirs_ref, behind, ahead), (mine_ref, ahead, behind)):
        for u in range(half):
            piece = lax.rem(jnp.where(my_core == 0, up[u], down[u]) + 2 * my_y, 2 * half)
            column = pl.multiple_of(piece * slab, slab)
            block = x_ref[:, pl.ds(column, slab)].astype(jnp.float32)
            scaled = block * gain_ref[:, pl.ds(column, slab)]
            out[:, u * slab : (u + 1) * slab] = scaled.astype(out.dtype)


def arrange(x, gain, slab):
    tokens, d_model = x.shape
    half = jax.ShapeDtypeStruct((tokens, d_model // CORES), x.dtype)
    vmem = pl.BlockSpec(memory_space=pltpu.VMEM)
    return pl.pallas_call(
        functools.partial(arrange_kernel, slab),
        out_shape=(half, half),
        in_specs=[vmem, vmem],
        out_specs=(vmem, vmem),
        cost_estimate=pl.CostEstimate(
            flops=tokens * d_model, bytes_accessed=4 * tokens * d_model, transcendentals=0
        ),
        compiler_params=pltpu.CompilerParams(vmem_limit_bytes=12 << 20),
        name="arrange",
    )(x, gain)


def products_kernel(slab, begin, after, x_ref, xg_ref, c_ref, cg_ref, *outs):
    dims = (((0,), (0,)), ((), ()))
    for u, out in enumerate(outs[after:], begin):
        cols = slice(u * slab, (u + 1) * slab)
        total = lax.dot_general(
            x_ref[:, cols], c_ref[...], dims, preferred_element_type=jnp.float32
        ) + lax.dot_general(
            xg_ref[:, cols], cg_ref[...], dims, preferred_element_type=jnp.float32
        )
        out[...] = total.astype(out.dtype)


def products(mine, got, cot, cot_got, slab, begin, end, *after):
    tokens, _ = mine.shape
    width = cot.shape[1]
    count = end - begin
    vmem = pl.BlockSpec(memory_space=pltpu.VMEM)
    return pl.pallas_call(
        functools.partial(products_kernel, slab, begin, len(after)),
        out_shape=tuple(jax.ShapeDtypeStruct((slab, width), cot.dtype) for _ in range(count)),
        in_specs=[vmem] * 4 + [pl.BlockSpec(memory_space=pl.ANY)] * len(after),
        out_specs=tuple([vmem] * count),
        cost_estimate=pl.CostEstimate(
            flops=4 * tokens * count * slab * width,
            bytes_accessed=4 * count * slab * width,
            transcendentals=0,
        ),
        compiler_params=pltpu.CompilerParams(vmem_limit_bytes=16 << 20),
        name="products",
    )(mine, got, cot, cot_got, *after)


def finish_kernel(a_ref, b_ref, out_ref):
    head = out_ref.shape[2]
    slab = a_ref.shape[0]
    for t in range(a_ref.shape[1] // head):
        cols = slice(t * head, (t + 1) * head)
        total = a_ref[:, cols].astype(jnp.float32) + b_ref[:, cols].astype(jnp.float32)
        x, row = divmod(t * slab, out_ref.shape[1])
        out_ref[x, row : row + slab, :] = total.astype(out_ref.dtype)


def finish(a, b, head):
    vmem = pl.BlockSpec(memory_space=pltpu.VMEM)
    return pl.pallas_call(
        finish_kernel,
        out_shape=jax.ShapeDtypeStruct((N_X, a.size // (N_X * head), head), a.dtype),
        in_specs=[vmem, vmem],
        out_specs=vmem,
        cost_estimate=pl.CostEstimate(
            flops=a.size, bytes_accessed=6 * a.size, transcendentals=0
        ),
        compiler_params=pltpu.CompilerParams(vmem_limit_bytes=8 << 20),
        name="finish",
    )(a, b)


def small_kernel(body, out_shape, *operands, scalars=0):
    vmem = pl.BlockSpec(memory_space=pltpu.VMEM)
    smem = pl.BlockSpec(memory_space=pltpu.SMEM)
    size = sum(a.size for a in operands)
    return pl.pallas_call(
        body,
        out_shape=out_shape,
        in_specs=[smem] * scalars + [vmem] * (len(operands) - scalars),
        out_specs=jax.tree.map(lambda _: vmem, out_shape),
        cost_estimate=pl.CostEstimate(flops=size, bytes_accessed=4 * size, transcendentals=0),
        compiler_params=pltpu.CompilerParams(vmem_limit_bytes=8 << 20),
    )(*operands)


def total_of(ref, rows=slice(None)):
    return sum(ref[j, rows, :].astype(jnp.float32) for j in range(ref.shape[0]))


def sum_x_kernel(rows, got_ref, out_ref):
    total = total_of(got_ref)
    full, head = total.shape
    for j in range(out_ref.shape[0]):
        begin, end = min(j * rows, full), min(j * rows + rows, full)
        fill = jnp.zeros((out_ref.shape[1] - end + begin, head), jnp.float32)
        block = jnp.concatenate([total[begin:end], fill], axis=0)
        out_ref[j] = block.astype(out_ref.dtype)


def sum_z_kernel(got_ref, extra_ref, out_ref):
    total = total_of(got_ref) + extra_ref[...].astype(jnp.float32)
    for j in range(out_ref.shape[0]):
        out_ref[j] = total.astype(out_ref.dtype)


def pack_kernel(rows, got_ref, out_ref, stats_ref):
    count, _, head = got_ref.shape
    pad = -count % 16
    full = out_ref.shape[0] - count - pad
    blocks = [got_ref[j].astype(jnp.float32) for j in range(count)]
    grad = jnp.concatenate([block[:rows] for block in blocks], axis=0)[:full]
    out_ref[:full, :] = grad.astype(out_ref.dtype)
    tail = [block[rows : rows + 1] for block in blocks] + [jnp.zeros((pad, head), jnp.float32)]
    out_ref[full:, :] = jnp.concatenate(tail, axis=0).astype(out_ref.dtype)
    squares = grad * grad
    half = full // 2
    stats = [jnp.sum(squares[t * half : (t + 1) * half], axis=0, keepdims=True) for t in range(2)]
    stats.append(sum(block[rows + 1 : rows + 2] for block in blocks))
    stats.append(jnp.zeros((stats_ref.shape[1] - 3, head), jnp.float32))
    stats = jnp.concatenate(stats, axis=0)
    for j in range(stats_ref.shape[0]):
        stats_ref[j] = stats


def update_kernel(index_ref, state_ref, pick_ref, lane_ref, *refs):
    *got, stats_ref, weight_ref, col_state_ref, out_ref, own_ref, col_ref = refs
    my_x = lax.axis_index("grp") % N_X
    tensors, head = col_ref.shape
    slab = weight_ref.shape[0]
    full = pick_ref.shape[0] // N_X
    plane = stats_ref.shape[0] // N_X
    d_model = slab * plane

    sums = jnp.sum(stats_ref[:, 2, :], axis=0, keepdims=True)
    factors = []
    for t in range(tensors):
        x = t // 2
        col = jnp.sum(stats_ref[x * plane : (x + 1) * plane, t % 2, :], axis=0, keepdims=True)
        col = col / d_model + epsilon
        col_new = decay_rate * col_state_ref[t : t + 1, :] + (1.0 - decay_rate) * col
        col_ref[t : t + 1, :] = col_new
        prev = (sums[:, t : t + 1] + sums[:, tensors + t : tensors + t + 1]) / d_model
        average = decay_rate * prev + (1.0 - decay_rate) * jnp.mean(col, axis=1, keepdims=True)
        factors.append(step_size * lax.rsqrt(col_new / average))

    states = jnp.concatenate([ref[full:, :] for ref in got], axis=0)
    for t in range(tensors):
        rows = slice((t % 2) * slab, (t % 2 + 1) * slab)
        grad = got[0][rows, :]
        for k in range(1, N_X):
            grad = jnp.where((my_x ^ k) == t // 2, got[k][rows, :], grad)
        grad = grad.astype(jnp.float32)
        where = slice(t * slab, (t + 1) * slab)
        state = jnp.dot(pick_ref[where, :], states, preferred_element_type=jnp.float32)
        prev = jnp.sum(state * lane_ref[where, :].astype(jnp.float32), axis=1, keepdims=True)
        mean = jnp.sum(grad * grad, axis=1, keepdims=True) / head + epsilon
        scale = lax.rsqrt(decay_rate * prev + (1.0 - decay_rate) * mean)
        cols = slice(t * head, (t + 1) * head)
        change = grad * scale * factors[t]
        out_ref[:, cols] = (weight_ref[:, cols].astype(jnp.float32) - change).astype(out_ref.dtype)

    capacity, unit_rows = own_ref.shape
    per_piece = full // unit_rows
    shape = (unit_rows, unit_rows)
    eye = lax.broadcasted_iota(jnp.int32, shape, 0) == lax.broadcasted_iota(jnp.int32, shape, 1)
    for c in range(capacity):
        unit = jnp.maximum(index_ref[c], 0)
        rows = pl.ds(pl.multiple_of((unit % per_piece) * unit_rows, unit_rows), unit_rows)
        grad = got[0][rows, :]
        for k in range(1, N_X):
            grad = jnp.where((my_x ^ k) == unit // per_piece, got[k][rows, :], grad)
        grad = grad.astype(jnp.float32)
        mean = jnp.sum(grad * grad, axis=1, keepdims=True) / head + epsilon
        mean = jnp.sum(jnp.where(eye, mean, 0.0), axis=0, keepdims=True)
        new = decay_rate * state_ref[c : c + 1, :] + (1.0 - decay_rate) * mean
        own_ref[c : c + 1, :] = jnp.where(index_ref[c] >= 0, new, 0.0)


def tables_kernel(row, owner_ref, state_ref, pick_ref, lane_ref, extra_ref, index_ref):
    f32, bf16 = jnp.float32, jnp.bfloat16
    me = lax.axis_index("grp")
    units = owner_ref.shape[0]
    capacity, unit_rows = state_ref.shape
    count, head = lane_ref.shape
    half = capacity * unit_rows
    tensors = units // unit_rows
    seats = pick_ref.shape[1]

    def at(shape, axis):
        return lax.broadcasted_iota(jnp.int32, shape, axis)

    owner = owner_ref[...]
    hot = (owner == at((units, head), 1)).astype(f32)
    earlier = (at((units, units), 1) < at((units, units), 0)).astype(bf16)
    before = jnp.dot(earlier, hot.astype(bf16), preferred_element_type=f32)
    slot = jnp.sum(before * hot, axis=1, keepdims=True).astype(jnp.int32)

    seat = ((owner ^ me) & (N_X - 1)) * (seats // N_X) + owner // N_X
    spread = ((at((count, units), 0) // unit_rows) == at((count, units), 1)).astype(bf16)
    hot = (seat == at((units, seats), 1)).astype(bf16)
    pick_ref[...] = jnp.dot(spread, hot, preferred_element_type=f32).astype(bf16)
    lanes = at((units, head), 1)
    hot = (slot == (lanes % half) // unit_rows).astype(bf16)
    match = (at((count, head), 0) % unit_rows) == (at((count, head), 1) % unit_rows)
    hot = jnp.dot(spread, hot, preferred_element_type=f32)
    lane_ref[...] = jnp.where(match, hot, 0.0).astype(bf16)

    state = state_ref[...]
    high = state.astype(bf16)
    low = (state - high.astype(f32)).astype(bf16)
    copies = (at((unit_rows, head), 0) == at((unit_rows, head), 1) % unit_rows).astype(bf16)
    high = jnp.dot(high, copies, preferred_element_type=f32)
    low = jnp.dot(low, copies, preferred_element_type=f32)
    lanes = at((capacity, head), 1)
    parts = jnp.where(lanes < half, high, low)
    mine = (lanes % half) // unit_rows == at((capacity, head), 0)
    state_row = jnp.sum(jnp.where(mine, parts, 0.0), axis=0, keepdims=True)
    number = at((units, 1), 0)
    sums = jnp.zeros((units, 1), f32)
    for c in range(capacity):
        here = (owner == me) & (slot == c)
        total = jnp.sum(state[c : c + 1, :], axis=1, keepdims=True)
        sums = sums + jnp.where(here, total, 0.0)
        index_ref[c] = jnp.max(jnp.where(here, number.astype(f32), -1.0)).astype(jnp.int32)
    lanes = at((units, head), 1)
    tensor = at((units, head), 0) // unit_rows
    here = (lanes % tensors == tensor) & (lanes < 2 * tensors)
    value = jnp.sum(jnp.where(here, sums, 0.0), axis=0, keepdims=True)
    high = value.astype(bf16).astype(f32)
    sum_row = jnp.where(at((1, head), 1) < tensors, high, value - high)
    at_row = at(extra_ref.shape, 0)
    extra = jnp.where(at_row == row, state_row, jnp.where(at_row == row + 1, sum_row, 0.0))
    extra_ref[...] = extra.astype(bf16)


def tables(owner_table, state, head, seats, row, rows):
    capacity, unit_rows = state.shape
    count = owner_table.shape[0] * unit_rows
    vmem = pl.BlockSpec(memory_space=pltpu.VMEM)
    smem = pl.BlockSpec(memory_space=pltpu.SMEM)
    bf16 = jnp.bfloat16
    return pl.pallas_call(
        functools.partial(tables_kernel, row),
        out_shape=(
            jax.ShapeDtypeStruct((count, seats), bf16),
            jax.ShapeDtypeStruct((count, head), bf16),
            jax.ShapeDtypeStruct((rows, head), bf16),
            jax.ShapeDtypeStruct((capacity,), jnp.int32),
        ),
        in_specs=[vmem, vmem],
        out_specs=(vmem, vmem, vmem, smem),
        cost_estimate=pl.CostEstimate(
            flops=count * head * 100, bytes_accessed=4 * count * head, transcendentals=0
        ),
        compiler_params=pltpu.CompilerParams(vmem_limit_bytes=8 << 20),
        name="tables",
    )(owner_table, state)


def on_device(normed, cotangent, norm_gain, weights, row_state, col_state, owner_table):
    bf16, f32 = jnp.bfloat16, jnp.float32
    groups = lax.axis_size("grp")
    intra = lax.axis_size("intra")
    n_y = intra // CORES
    n_z = groups // N_X
    tensors, head = col_state.shape
    capacity, unit_rows = row_state.shape[2:]
    slab = weights.shape[0]
    blocks = slab // unit_rows
    units = tensors * blocks

    x_groups = [[z * N_X + x for x in range(N_X)] for z in range(n_z)]
    z_groups = [[z * N_X + x for z in range(n_z)] for x in range(N_X)]


    swap = [(i, i ^ 1) for i in range(intra)]
    cot_got = lax.ppermute(cotangent, "intra", swap)
    mine, theirs = arrange(normed, norm_gain[None, :], slab)
    got = lax.ppermute(theirs, "intra", swap)
    inputs = (mine, got, cotangent, cot_got, slab)
    parts = products(*inputs, 0, 1)
    parts = parts + products(*inputs, 1, mine.shape[1] // slab, parts[0])

    ring = [
        (y * CORES + c, ((y + 1 - 2 * c) % n_y) * CORES + c) for y in range(n_y) for c in range(CORES)
    ]

    def add(*terms):
        return sum(t.astype(f32) for t in terms)

    def hop(a):
        return lax.ppermute(a, "intra", ring)

    first, second = parts[0], parts[2]
    for k in range(1, len(parts) - 2, 2):
        first = add(hop(first), parts[k]).astype(bf16)
        if k > 1:
            second = add(hop(second), parts[k + 1]).astype(bf16)
    last = hop(first)
    give = add(hop(second), parts[-1]).astype(bf16)
    other = lax.ppermute(give, "intra", swap)
    state_rows = n_z + -n_z % unit_rows
    per_x = units // N_X
    full = per_x * unit_rows
    share = -(-full // (4 * n_z)) * 4
    sent_rows = -(-(share + 2) // unit_rows) * unit_rows
    pick, lane, extra, my_index = tables(
        owner_table, row_state[0, 0], head, N_X * state_rows, share, sent_rows
    )
    last, other, extra, pick, lane, my_index = lax.optimization_barrier(
        (last, other, extra, pick, lane, my_index)
    )
    own = finish(last, other, head)


    got = lax.all_to_all(own, "grp", 0, 0, axis_index_groups=x_groups, tiled=True)
    block = jax.ShapeDtypeStruct((n_z, sent_rows, head), bf16)
    sent = small_kernel(functools.partial(sum_x_kernel, share), block, got)
    got = lax.all_to_all(sent, "grp", 0, 0, axis_index_groups=z_groups, tiled=True)

    sent = small_kernel(sum_z_kernel, block, got, extra)
    got = lax.all_to_all(sent, "grp", 0, 0, axis_index_groups=z_groups, tiled=True)
    shapes = (
        jax.ShapeDtypeStruct((full + state_rows, head), bf16),
        jax.ShapeDtypeStruct((N_X * intra, 8, head), f32),
    )
    body = functools.partial(pack_kernel, share)
    sent, stats = small_kernel(body, shapes, got)
    plane = N_X * intra
    planes = [list(range(z * plane, (z + 1) * plane)) for z in range(n_z)]
    stats = lax.all_to_all(
        stats, ("grp", "intra"), 0, 0, axis_index_groups=planes, tiled=True
    )

    def trade(a, k):
        pairs = [(g, g ^ k) for g in range(groups)]
        return lax.ppermute(a, "grp", pairs)

    near, wrap = trade(sent, 1), trade(sent, N_X - 1)
    fetched = [sent, near, trade(near, N_X - 1), wrap]

    shapes = (
        jax.ShapeDtypeStruct(weights.shape, weights.dtype),
        jax.ShapeDtypeStruct((capacity, unit_rows), f32),
        jax.ShapeDtypeStruct(col_state.shape, f32),
    )
    new_weights, row_moments, col_new = small_kernel(
        update_kernel,
        shapes,
        my_index,
        row_state[0, 0],
        pick,
        lane,
        *fetched,
        stats,
        weights,
        col_state,
        scalars=1,
    )
    return (new_weights, row_moments[None, None], col_new)


def solution(mesh):
    placed = (
        P(("grp", "intra"), None),
        P(("grp", "intra"), None),
        P(),
        P("intra", None),
        P("grp", "intra", None, None),
        P(),
        P(),
    )
    return jax.shard_map(
        on_device,
        mesh=mesh,
        in_specs=placed,
        out_specs=(P("intra", None), P("grp", "intra", None, None), P()),
        check_vma=False,
    )
```

```python
import functools

import jax
import jax.numpy as jnp
from jax import lax
from jax.experimental import pallas as pl
from jax.experimental.pallas import tpu as pltpu
from jax.sharding import PartitionSpec as P


decay_rate = 0.8
step_size = 0.5
epsilon = 1e-06

N_X = 4
CORES = 2


def arrange_kernel(slab, x_ref, gain_ref, mine_ref, theirs_ref):
    me = lax.axis_index("intra")
    my_y, my_core = me // CORES, me % CORES
    half = x_ref.shape[1] // (CORES * slab)
    n_y = 2 * half // CORES
    ahead = [n_y] + [2 * k + h for k in range(n_y // 2 - 1, 0, -1) for h in (0, 1)] + [1]
    behind = [n_y + 1] + [2 * k + h for k in range(n_y // 2 + 1, n_y) for h in (1, 0)] + [0]
    for out, up, down in ((theirs_ref, behind, ahead), (mine_ref, ahead, behind)):
        for u in range(half):
            piece = lax.rem(jnp.where(my_core == 0, up[u], down[u]) + 2 * my_y, 2 * half)
            column = pl.multiple_of(piece * slab, slab)
            block = x_ref[:, pl.ds(column, slab)].astype(jnp.float32)
            scaled = block * gain_ref[:, pl.ds(column, slab)]
            out[:, u * slab : (u + 1) * slab] = scaled.astype(out.dtype)


def arrange(x, gain, slab):
    tokens, d_model = x.shape
    half = jax.ShapeDtypeStruct((tokens, d_model // CORES), x.dtype)
    vmem = pl.BlockSpec(memory_space=pltpu.VMEM)
    return pl.pallas_call(
        functools.partial(arrange_kernel, slab),
        out_shape=(half, half),
        in_specs=[vmem, vmem],
        out_specs=(vmem, vmem),
        cost_estimate=pl.CostEstimate(
            flops=tokens * d_model, bytes_accessed=4 * tokens * d_model, transcendentals=0
        ),
        compiler_params=pltpu.CompilerParams(vmem_limit_bytes=12 << 20),
        name="arrange",
    )(x, gain)


def products_kernel(slab, begin, after, x_ref, xg_ref, c_ref, cg_ref, *outs):
    dims = (((0,), (0,)), ((), ()))
    for u, out in enumerate(outs[after:], begin):
        cols = slice(u * slab, (u + 1) * slab)
        total = lax.dot_general(
            x_ref[:, cols], c_ref[...], dims, preferred_element_type=jnp.float32
        ) + lax.dot_general(
            xg_ref[:, cols], cg_ref[...], dims, preferred_element_type=jnp.float32
        )
        out[...] = total.astype(out.dtype)


def products(mine, got, cot, cot_got, slab, begin, end, *after):
    tokens, _ = mine.shape
    width = cot.shape[1]
    count = end - begin
    vmem = pl.BlockSpec(memory_space=pltpu.VMEM)
    return pl.pallas_call(
        functools.partial(products_kernel, slab, begin, len(after)),
        out_shape=tuple(jax.ShapeDtypeStruct((slab, width), cot.dtype) for _ in range(count)),
        in_specs=[vmem] * 4 + [pl.BlockSpec(memory_space=pl.ANY)] * len(after),
        out_specs=tuple([vmem] * count),
        cost_estimate=pl.CostEstimate(
            flops=4 * tokens * count * slab * width,
            bytes_accessed=4 * count * slab * width,
            transcendentals=0,
        ),
        compiler_params=pltpu.CompilerParams(vmem_limit_bytes=16 << 20),
        name="products",
    )(mine, got, cot, cot_got, *after)


def finish_kernel(a_ref, b_ref, out_ref):
    head = out_ref.shape[2]
    slab = a_ref.shape[0]
    for t in range(a_ref.shape[1] // head):
        cols = slice(t * head, (t + 1) * head)
        total = a_ref[:, cols].astype(jnp.float32) + b_ref[:, cols].astype(jnp.float32)
        x, row = divmod(t * slab, out_ref.shape[1])
        out_ref[x, row : row + slab, :] = total.astype(out_ref.dtype)


def finish(a, b, head):
    vmem = pl.BlockSpec(memory_space=pltpu.VMEM)
    return pl.pallas_call(
        finish_kernel,
        out_shape=jax.ShapeDtypeStruct((N_X, a.size // (N_X * head), head), a.dtype),
        in_specs=[vmem, vmem],
        out_specs=vmem,
        cost_estimate=pl.CostEstimate(
            flops=a.size, bytes_accessed=6 * a.size, transcendentals=0
        ),
        compiler_params=pltpu.CompilerParams(vmem_limit_bytes=8 << 20),
        name="finish",
    )(a, b)


def small_kernel(body, out_shape, *operands, scalars=0):
    vmem = pl.BlockSpec(memory_space=pltpu.VMEM)
    smem = pl.BlockSpec(memory_space=pltpu.SMEM)
    size = sum(a.size for a in operands)
    return pl.pallas_call(
        body,
        out_shape=out_shape,
        in_specs=[smem] * scalars + [vmem] * (len(operands) - scalars),
        out_specs=jax.tree.map(lambda _: vmem, out_shape),
        cost_estimate=pl.CostEstimate(flops=size, bytes_accessed=4 * size, transcendentals=0),
        compiler_params=pltpu.CompilerParams(vmem_limit_bytes=8 << 20),
    )(*operands)


def total_of(ref, rows=slice(None)):
    return sum(ref[j, rows, :].astype(jnp.float32) for j in range(ref.shape[0]))


def sum_x_kernel(rows, got_ref, out_ref):
    total = total_of(got_ref)
    full, head = total.shape
    for j in range(out_ref.shape[0]):
        begin, end = min(j * rows, full), min(j * rows + rows, full)
        fill = jnp.zeros((out_ref.shape[1] - end + begin, head), jnp.float32)
        block = jnp.concatenate([total[begin:end], fill], axis=0)
        out_ref[j] = block.astype(out_ref.dtype)


def sum_z_kernel(got_ref, extra_ref, out_ref):
    total = total_of(got_ref) + extra_ref[...].astype(jnp.float32)
    for j in range(out_ref.shape[0]):
        out_ref[j] = total.astype(out_ref.dtype)


def pack_kernel(rows, got_ref, out_ref):
    count, _, head = got_ref.shape
    pad = -count % 16
    full = out_ref.shape[1] - count - pad
    blocks = [got_ref[j].astype(jnp.float32) for j in range(count)]
    grad = jnp.concatenate([block[:rows] for block in blocks], axis=0)[:full]
    grad = grad.astype(out_ref.dtype)
    sums = sum(block[rows + 1 : rows + 2] for block in blocks)
    high = sums.astype(out_ref.dtype).astype(jnp.float32)
    tail = [block[rows : rows + 1] for block in blocks] + [high, sums - high]
    tail = jnp.concatenate(tail + [jnp.zeros((pad - 2, head), jnp.float32)], axis=0)
    for x in range(out_ref.shape[0]):
        out_ref[x, :full, :] = grad
        out_ref[x, full:, :] = tail.astype(out_ref.dtype)


def stats_kernel(count, full, got_ref, out_ref):
    half = full // 2
    rows = []
    for x in range(got_ref.shape[0]):
        for t in range(2):
            grad = got_ref[x, t * half : (t + 1) * half, :].astype(jnp.float32)
            rows.append(jnp.sum(grad * grad, axis=0, keepdims=True))
    tails = [got_ref[x, full:, :].astype(jnp.float32) for x in range(got_ref.shape[0])]
    rows.append(sum(t[count : count + 1] + t[count + 1 : count + 2] for t in tails))
    fill = out_ref.shape[0] - len(rows)
    rows.append(jnp.zeros((fill, out_ref.shape[1]), jnp.float32))
    out_ref[...] = jnp.concatenate(rows, axis=0)


def both_kernel(a_ref, b_ref, out_ref):
    total = a_ref[...] + b_ref[...]
    for j in range(out_ref.shape[0]):
        out_ref[j] = total


def rows_kernel(index_ref, state_ref, pick_ref, lane_ref, got_ref, out_ref, own_ref):
    n_x, _, head = got_ref.shape
    full = pick_ref.shape[0] // n_x
    slab = full // 2
    states = jnp.concatenate([got_ref[x, full:, :] for x in range(n_x)], axis=0)
    for t in range(2 * n_x):
        grad = got_ref[t // 2, (t % 2) * slab : (t % 2 + 1) * slab, :].astype(jnp.float32)
        where = slice(t * slab, (t + 1) * slab)
        state = jnp.dot(pick_ref[where, :], states, preferred_element_type=jnp.float32)
        prev = jnp.sum(state * lane_ref[where, :].astype(jnp.float32), axis=1, keepdims=True)
        mean = jnp.sum(grad * grad, axis=1, keepdims=True) / head + epsilon
        out_ref[where, :] = grad * lax.rsqrt(decay_rate * prev + (1.0 - decay_rate) * mean)

    capacity, unit_rows = own_ref.shape
    per_piece = full // unit_rows
    shape = (unit_rows, unit_rows)
    eye = lax.broadcasted_iota(jnp.int32, shape, 0) == lax.broadcasted_iota(jnp.int32, shape, 1)
    for c in range(capacity):
        unit = jnp.maximum(index_ref[c], 0)
        rows = pl.ds(pl.multiple_of((unit % per_piece) * unit_rows, unit_rows), unit_rows)
        grad = got_ref[0, rows, :]
        for x in range(1, n_x):
            grad = jnp.where(unit // per_piece == x, got_ref[x, rows, :], grad)
        grad = grad.astype(jnp.float32)
        mean = jnp.sum(grad * grad, axis=1, keepdims=True) / head + epsilon
        mean = jnp.sum(jnp.where(eye, mean, 0.0), axis=0, keepdims=True)
        new = decay_rate * state_ref[c : c + 1, :] + (1.0 - decay_rate) * mean
        own_ref[c : c + 1, :] = jnp.where(index_ref[c] >= 0, new, 0.0)


def update_kernel(stats_ref, grad_ref, weight_ref, state_ref, out_ref, col_ref):
    tensors, head = state_ref.shape
    slab = weight_ref.shape[0]
    d_model = CORES * slab * stats_ref.shape[0]
    total = sum(stats_ref[j] for j in range(stats_ref.shape[0])) / d_model
    for t in range(tensors):
        col = total[t : t + 1] + epsilon
        col_new = decay_rate * state_ref[t : t + 1, :] + (1.0 - decay_rate) * col
        col_ref[t : t + 1, :] = col_new
        sums = total[tensors : tensors + 1]
        prev = sums[:, t : t + 1] + sums[:, tensors + t : tensors + t + 1]
        average = decay_rate * prev + (1.0 - decay_rate) * jnp.mean(col, axis=1, keepdims=True)
        factor = step_size * lax.rsqrt(col_new / average)
        cols = slice(t * head, (t + 1) * head)
        change = grad_ref[t * slab : (t + 1) * slab, :] * factor
        out_ref[:, cols] = (weight_ref[:, cols].astype(jnp.float32) - change).astype(out_ref.dtype)


def tables_kernel(row, owner_ref, state_ref, pick_ref, lane_ref, extra_ref, index_ref):
    f32, bf16 = jnp.float32, jnp.bfloat16
    me = lax.axis_index("grp")
    units = owner_ref.shape[0]
    capacity, unit_rows = state_ref.shape
    count, head = lane_ref.shape
    half = capacity * unit_rows
    tensors = units // unit_rows
    seats = pick_ref.shape[1]

    def at(shape, axis):
        return lax.broadcasted_iota(jnp.int32, shape, axis)

    owner = owner_ref[...]
    hot = (owner == at((units, head), 1)).astype(f32)
    earlier = (at((units, units), 1) < at((units, units), 0)).astype(bf16)
    before = jnp.dot(earlier, hot.astype(bf16), preferred_element_type=f32)
    slot = jnp.sum(before * hot, axis=1, keepdims=True).astype(jnp.int32)

    seat = (owner % N_X) * (seats // N_X) + owner // N_X
    spread = ((at((count, units), 0) // unit_rows) == at((count, units), 1)).astype(bf16)
    hot = (seat == at((units, seats), 1)).astype(bf16)
    pick_ref[...] = jnp.dot(spread, hot, preferred_element_type=f32).astype(bf16)
    lanes = at((units, head), 1)
    hot = (slot == (lanes % half) // unit_rows).astype(bf16)
    match = (at((count, head), 0) % unit_rows) == (at((count, head), 1) % unit_rows)
    hot = jnp.dot(spread, hot, preferred_element_type=f32)
    lane_ref[...] = jnp.where(match, hot, 0.0).astype(bf16)

    state = state_ref[...]
    high = state.astype(bf16)
    low = (state - high.astype(f32)).astype(bf16)
    copies = (at((unit_rows, head), 0) == at((unit_rows, head), 1) % unit_rows).astype(bf16)
    high = jnp.dot(high, copies, preferred_element_type=f32)
    low = jnp.dot(low, copies, preferred_element_type=f32)
    lanes = at((capacity, head), 1)
    parts = jnp.where(lanes < half, high, low)
    mine = (lanes % half) // unit_rows == at((capacity, head), 0)
    state_row = jnp.sum(jnp.where(mine, parts, 0.0), axis=0, keepdims=True)
    number = at((units, 1), 0)
    sums = jnp.zeros((units, 1), f32)
    for c in range(capacity):
        here = (owner == me) & (slot == c)
        total = jnp.sum(state[c : c + 1, :], axis=1, keepdims=True)
        sums = sums + jnp.where(here, total, 0.0)
        index_ref[c] = jnp.max(jnp.where(here, number.astype(f32), -1.0)).astype(jnp.int32)
    lanes = at((units, head), 1)
    tensor = at((units, head), 0) // unit_rows
    here = (lanes % tensors == tensor) & (lanes < 2 * tensors)
    value = jnp.sum(jnp.where(here, sums, 0.0), axis=0, keepdims=True)
    high = value.astype(bf16).astype(f32)
    sum_row = jnp.where(at((1, head), 1) < tensors, high, value - high)
    at_row = at(extra_ref.shape, 0)
    extra = jnp.where(at_row == row, state_row, jnp.where(at_row == row + 1, sum_row, 0.0))
    extra_ref[...] = extra.astype(bf16)


def tables(owner_table, state, head, seats, row, rows):
    capacity, unit_rows = state.shape
    count = owner_table.shape[0] * unit_rows
    vmem = pl.BlockSpec(memory_space=pltpu.VMEM)
    smem = pl.BlockSpec(memory_space=pltpu.SMEM)
    bf16 = jnp.bfloat16
    return pl.pallas_call(
        functools.partial(tables_kernel, row),
        out_shape=(
            jax.ShapeDtypeStruct((count, seats), bf16),
            jax.ShapeDtypeStruct((count, head), bf16),
            jax.ShapeDtypeStruct((rows, head), bf16),
            jax.ShapeDtypeStruct((capacity,), jnp.int32),
        ),
        in_specs=[vmem, vmem],
        out_specs=(vmem, vmem, vmem, smem),
        cost_estimate=pl.CostEstimate(
            flops=count * head * 100, bytes_accessed=4 * count * head, transcendentals=0
        ),
        compiler_params=pltpu.CompilerParams(vmem_limit_bytes=8 << 20),
        name="tables",
    )(owner_table, state)


def on_device(normed, cotangent, norm_gain, weights, row_state, col_state, owner_table):
    bf16, f32 = jnp.bfloat16, jnp.float32
    groups = lax.axis_size("grp")
    intra = lax.axis_size("intra")
    n_y = intra // CORES
    n_z = groups // N_X
    tensors, head = col_state.shape
    capacity, unit_rows = row_state.shape[2:]
    slab = weights.shape[0]
    blocks = slab // unit_rows
    units = tensors * blocks

    same_core = [[y * CORES + c for y in range(n_y)] for c in range(CORES)]
    x_groups = [[z * N_X + x for x in range(N_X)] for z in range(n_z)]
    z_groups = [[z * N_X + x for z in range(n_z)] for x in range(N_X)]


    swap = [(i, i ^ 1) for i in range(intra)]
    cot_got = lax.ppermute(cotangent, "intra", swap)
    mine, theirs = arrange(normed, norm_gain[None, :], slab)
    got = lax.ppermute(theirs, "intra", swap)
    inputs = (mine, got, cotangent, cot_got, slab)
    parts = products(*inputs, 0, 1)
    parts = parts + products(*inputs, 1, mine.shape[1] // slab, parts[0])

    ring = [
        (y * CORES + c, ((y + 1 - 2 * c) % n_y) * CORES + c) for y in range(n_y) for c in range(CORES)
    ]

    def add(*terms):
        return sum(t.astype(f32) for t in terms)

    def hop(a):
        return lax.ppermute(a, "intra", ring)

    first, second = parts[0], parts[2]
    for k in range(1, len(parts) - 2, 2):
        first = add(hop(first), parts[k]).astype(bf16)
        if k > 1:
            second = add(hop(second), parts[k + 1]).astype(bf16)
    last = hop(first)
    give = add(hop(second), parts[-1]).astype(bf16)
    other = lax.ppermute(give, "intra", swap)
    state_rows = n_z + -n_z % unit_rows
    per_x = units // N_X
    full = per_x * unit_rows
    share = -(-full // (4 * n_z)) * 4
    sent_rows = -(-(share + 2) // unit_rows) * unit_rows
    pick, lane, extra, my_index = tables(
        owner_table, row_state[0, 0], head, N_X * state_rows, share, sent_rows
    )
    last, other, extra, pick, lane, my_index = lax.optimization_barrier(
        (last, other, extra, pick, lane, my_index)
    )
    own = finish(last, other, head)


    got = lax.all_to_all(own, "grp", 0, 0, axis_index_groups=x_groups, tiled=True)
    block = jax.ShapeDtypeStruct((n_z, sent_rows, head), bf16)
    sent = small_kernel(functools.partial(sum_x_kernel, share), block, got)
    got = lax.all_to_all(sent, "grp", 0, 0, axis_index_groups=z_groups, tiled=True)

    sent = small_kernel(sum_z_kernel, block, got, extra)
    got = lax.all_to_all(sent, "grp", 0, 0, axis_index_groups=z_groups, tiled=True)
    sent = jax.ShapeDtypeStruct((N_X, full + state_rows, head), bf16)
    sent = small_kernel(functools.partial(pack_kernel, share), sent, got)
    got = lax.all_to_all(sent, "grp", 0, 0, axis_index_groups=x_groups, tiled=True)

    stats = jax.ShapeDtypeStruct((2 * tensors, head), f32)
    stats = small_kernel(functools.partial(stats_kernel, n_z, full), stats, got)
    partner = lax.ppermute(stats, "intra", swap)
    shapes = (
        jax.ShapeDtypeStruct((units * unit_rows, head), f32),
        jax.ShapeDtypeStruct((capacity, unit_rows), f32),
    )
    scaled, row_moments = small_kernel(
        rows_kernel, shapes, my_index, row_state[0, 0], pick, lane, got, scalars=1
    )
    sent = jax.ShapeDtypeStruct((n_y,) + stats.shape, f32)
    sent = small_kernel(both_kernel, sent, stats, partner)
    stats = lax.all_to_all(sent, "intra", 0, 0, axis_index_groups=same_core, tiled=True)
    shapes = (
        jax.ShapeDtypeStruct(weights.shape, weights.dtype),
        jax.ShapeDtypeStruct(col_state.shape, f32),
    )
    new_weights, col_new = small_kernel(update_kernel, shapes, stats, scaled, weights, col_state)
    return (new_weights, row_moments[None, None], col_new)


def solution(mesh):
    placed = (
        P(("grp", "intra"), None),
        P(("grp", "intra"), None),
        P(),
        P("intra", None),
        P("grp", "intra", None, None),
        P(),
        P(),
    )
    return jax.shard_map(
        on_device,
        mesh=mesh,
        in_specs=placed,
        out_specs=(P("intra", None), P("grp", "intra", None, None), P()),
        check_vma=False,
    )
```

```python
import functools

import jax
import jax.numpy as jnp
from jax import lax
from jax.experimental import pallas as pl
from jax.experimental.pallas import tpu as pltpu
from jax.sharding import PartitionSpec as P


decay_rate = 0.8
step_size = 0.5
epsilon = 1e-06

N_X = 4
CORES = 2


def arrange_kernel(slab, x_ref, gain_ref, cot_ref, mine_ref, theirs_ref):
    me = lax.axis_index("intra")
    my_y, my_core = me // CORES, me % CORES
    half = x_ref.shape[1] // (CORES * slab)
    n_y = 2 * half // CORES
    ahead = [n_y] + [2 * k + h for k in range(n_y // 2 - 1, 0, -1) for h in (0, 1)] + [1]
    behind = [n_y + 1] + [2 * k + h for k in range(n_y // 2 + 1, n_y) for h in (1, 0)] + [0]
    for out, up, down in ((theirs_ref, behind, ahead), (mine_ref, ahead, behind)):
        for u in range(half):
            piece = lax.rem(jnp.where(my_core == 0, up[u], down[u]) + 2 * my_y, 2 * half)
            column = pl.multiple_of(piece * slab, slab)
            block = x_ref[:, pl.ds(column, slab)].astype(jnp.float32)
            scaled = block * gain_ref[:, pl.ds(column, slab)]
            out[:, u * slab : (u + 1) * slab] = scaled.astype(out.dtype)
    theirs_ref[:, half * slab :] = cot_ref[...]


def arrange(x, gain, cot, slab):
    tokens, d_model = x.shape
    half = d_model // CORES
    vmem = pl.BlockSpec(memory_space=pltpu.VMEM)
    return pl.pallas_call(
        functools.partial(arrange_kernel, slab),
        out_shape=(
            jax.ShapeDtypeStruct((tokens, half), x.dtype),
            jax.ShapeDtypeStruct((tokens, half + cot.shape[1]), x.dtype),
        ),
        in_specs=[vmem, vmem, vmem],
        out_specs=(vmem, vmem),
        cost_estimate=pl.CostEstimate(
            flops=tokens * d_model, bytes_accessed=4 * tokens * d_model, transcendentals=0
        ),
        compiler_params=pltpu.CompilerParams(vmem_limit_bytes=12 << 20),
        name="arrange",
    )(x, gain, cot)


def products_kernel(slab, pieces, after, x_ref, got_ref, c_ref, *outs):
    dims = (((0,), (0,)), ((), ()))
    rows = x_ref.shape[1]
    for u, out in zip(pieces, outs[after:]):
        cols = slice(u * slab, (u + 1) * slab)
        total = lax.dot_general(
            x_ref[:, cols], c_ref[...], dims, preferred_element_type=jnp.float32
        ) + lax.dot_general(
            got_ref[:, cols], got_ref[:, rows:], dims, preferred_element_type=jnp.float32
        )
        out[...] = total.astype(out.dtype)


def products(mine, got, cot, slab, pieces, *after):
    tokens = mine.shape[0]
    width = cot.shape[1]
    size = len(pieces) * slab * width
    vmem = pl.BlockSpec(memory_space=pltpu.VMEM)
    return pl.pallas_call(
        functools.partial(products_kernel, slab, pieces, len(after)),
        out_shape=tuple(jax.ShapeDtypeStruct((slab, width), cot.dtype) for _ in pieces),
        in_specs=[vmem] * 3 + [pl.BlockSpec(memory_space=pl.ANY)] * len(after),
        out_specs=tuple([vmem] * len(pieces)),
        cost_estimate=pl.CostEstimate(
            flops=4 * tokens * size, bytes_accessed=4 * size, transcendentals=0
        ),
        compiler_params=pltpu.CompilerParams(vmem_limit_bytes=16 << 20),
        name="products",
    )(mine, got, cot, *after)


def finish_kernel(a_ref, b_ref, out_ref):
    head = out_ref.shape[2]
    slab = a_ref.shape[0]
    for t in range(a_ref.shape[1] // head):
        cols = slice(t * head, (t + 1) * head)
        total = a_ref[:, cols].astype(jnp.float32) + b_ref[:, cols].astype(jnp.float32)
        x, row = divmod(t * slab, out_ref.shape[1])
        out_ref[x, row : row + slab, :] = total.astype(out_ref.dtype)


def finish(a, b, head):
    vmem = pl.BlockSpec(memory_space=pltpu.VMEM)
    return pl.pallas_call(
        finish_kernel,
        out_shape=jax.ShapeDtypeStruct((N_X, a.size // (N_X * head), head), a.dtype),
        in_specs=[vmem, vmem],
        out_specs=vmem,
        cost_estimate=pl.CostEstimate(
            flops=a.size, bytes_accessed=6 * a.size, transcendentals=0
        ),
        compiler_params=pltpu.CompilerParams(vmem_limit_bytes=8 << 20),
        name="finish",
    )(a, b)


def small_kernel(body, out_shape, *operands, scalars=0):
    vmem = pl.BlockSpec(memory_space=pltpu.VMEM)
    smem = pl.BlockSpec(memory_space=pltpu.SMEM)
    size = sum(a.size for a in operands)
    return pl.pallas_call(
        body,
        out_shape=out_shape,
        in_specs=[smem] * scalars + [vmem] * (len(operands) - scalars),
        out_specs=jax.tree.map(lambda _: vmem, out_shape),
        cost_estimate=pl.CostEstimate(flops=size, bytes_accessed=4 * size, transcendentals=0),
        compiler_params=pltpu.CompilerParams(vmem_limit_bytes=8 << 20),
    )(*operands)


def total_of(ref, rows=slice(None)):
    return sum(ref[j, rows, :].astype(jnp.float32) for j in range(ref.shape[0]))


def sum_x_kernel(rows, got_ref, out_ref):
    total = total_of(got_ref)
    full, head = total.shape
    for j in range(out_ref.shape[0]):
        begin, end = min(j * rows, full), min(j * rows + rows, full)
        fill = jnp.zeros((out_ref.shape[1] - end + begin, head), jnp.float32)
        block = jnp.concatenate([total[begin:end], fill], axis=0)
        out_ref[j] = block.astype(out_ref.dtype)


def sum_z_kernel(got_ref, extra_ref, out_ref):
    total = total_of(got_ref) + extra_ref[...].astype(jnp.float32)
    for j in range(out_ref.shape[0]):
        out_ref[j] = total.astype(out_ref.dtype)


def pack_kernel(rows, got_ref, out_ref):
    count, _, head = got_ref.shape
    pad = -count % 16
    full = out_ref.shape[1] - count - pad
    blocks = [got_ref[j].astype(jnp.float32) for j in range(count)]
    grad = jnp.concatenate([block[:rows] for block in blocks], axis=0)[:full]
    grad = grad.astype(out_ref.dtype)
    sums = sum(block[rows + 1 : rows + 2] for block in blocks)
    high = sums.astype(out_ref.dtype).astype(jnp.float32)
    tail = [block[rows : rows + 1] for block in blocks] + [high, sums - high]
    tail = jnp.concatenate(tail + [jnp.zeros((pad - 2, head), jnp.float32)], axis=0)
    for x in range(out_ref.shape[0]):
        out_ref[x, :full, :] = grad
        out_ref[x, full:, :] = tail.astype(out_ref.dtype)


def stats_kernel(count, full, got_ref, out_ref):
    half = full // 2
    rows = []
    for x in range(got_ref.shape[0]):
        for t in range(2):
            grad = got_ref[x, t * half : (t + 1) * half, :].astype(jnp.float32)
            rows.append(jnp.sum(grad * grad, axis=0, keepdims=True))
    tails = [got_ref[x, full:, :].astype(jnp.float32) for x in range(got_ref.shape[0])]
    rows.append(sum(t[count : count + 1] + t[count + 1 : count + 2] for t in tails))
    fill = out_ref.shape[0] - len(rows)
    rows.append(jnp.zeros((fill, out_ref.shape[1]), jnp.float32))
    out_ref[...] = jnp.concatenate(rows, axis=0)


def both_kernel(a_ref, b_ref, out_ref):
    total = a_ref[...] + b_ref[...]
    for j in range(out_ref.shape[0]):
        out_ref[j] = total


def rows_kernel(index_ref, state_ref, pick_ref, lane_ref, got_ref, out_ref, own_ref):
    n_x, _, head = got_ref.shape
    full = pick_ref.shape[0] // n_x
    slab = full // 2
    states = jnp.concatenate([got_ref[x, full:, :] for x in range(n_x)], axis=0)
    for t in range(2 * n_x):
        grad = got_ref[t // 2, (t % 2) * slab : (t % 2 + 1) * slab, :].astype(jnp.float32)
        where = slice(t * slab, (t + 1) * slab)
        state = jnp.dot(pick_ref[where, :], states, preferred_element_type=jnp.float32)
        prev = jnp.sum(state * lane_ref[where, :].astype(jnp.float32), axis=1, keepdims=True)
        mean = jnp.sum(grad * grad, axis=1, keepdims=True) / head + epsilon
        out_ref[where, :] = grad * lax.rsqrt(decay_rate * prev + (1.0 - decay_rate) * mean)

    capacity, unit_rows = own_ref.shape
    per_piece = full // unit_rows
    shape = (unit_rows, unit_rows)
    eye = lax.broadcasted_iota(jnp.int32, shape, 0) == lax.broadcasted_iota(jnp.int32, shape, 1)
    for c in range(capacity):
        unit = jnp.maximum(index_ref[c], 0)
        rows = pl.ds(pl.multiple_of((unit % per_piece) * unit_rows, unit_rows), unit_rows)
        grad = got_ref[0, rows, :]
        for x in range(1, n_x):
            grad = jnp.where(unit // per_piece == x, got_ref[x, rows, :], grad)
        grad = grad.astype(jnp.float32)
        mean = jnp.sum(grad * grad, axis=1, keepdims=True) / head + epsilon
        mean = jnp.sum(jnp.where(eye, mean, 0.0), axis=0, keepdims=True)
        new = decay_rate * state_ref[c : c + 1, :] + (1.0 - decay_rate) * mean
        own_ref[c : c + 1, :] = jnp.where(index_ref[c] >= 0, new, 0.0)


def update_kernel(stats_ref, grad_ref, weight_ref, state_ref, out_ref, col_ref):
    tensors, head = state_ref.shape
    slab = weight_ref.shape[0]
    d_model = CORES * slab * stats_ref.shape[0]
    total = sum(stats_ref[j] for j in range(stats_ref.shape[0])) / d_model
    for t in range(tensors):
        col = total[t : t + 1] + epsilon
        col_new = decay_rate * state_ref[t : t + 1, :] + (1.0 - decay_rate) * col
        col_ref[t : t + 1, :] = col_new
        sums = total[tensors : tensors + 1]
        prev = sums[:, t : t + 1] + sums[:, tensors + t : tensors + t + 1]
        average = decay_rate * prev + (1.0 - decay_rate) * jnp.mean(col, axis=1, keepdims=True)
        factor = step_size * lax.rsqrt(col_new / average)
        cols = slice(t * head, (t + 1) * head)
        change = grad_ref[t * slab : (t + 1) * slab, :] * factor
        out_ref[:, cols] = (weight_ref[:, cols].astype(jnp.float32) - change).astype(out_ref.dtype)


def tables_kernel(row, owner_ref, state_ref, pick_ref, lane_ref, extra_ref, index_ref):
    f32, bf16 = jnp.float32, jnp.bfloat16
    me = lax.axis_index("grp")
    units = owner_ref.shape[0]
    capacity, unit_rows = state_ref.shape
    count, head = lane_ref.shape
    half = capacity * unit_rows
    tensors = units // unit_rows
    seats = pick_ref.shape[1]

    def at(shape, axis):
        return lax.broadcasted_iota(jnp.int32, shape, axis)

    owner = owner_ref[...]
    hot = (owner == at((units, head), 1)).astype(f32)
    earlier = (at((units, units), 1) < at((units, units), 0)).astype(bf16)
    before = jnp.dot(earlier, hot.astype(bf16), preferred_element_type=f32)
    slot = jnp.sum(before * hot, axis=1, keepdims=True).astype(jnp.int32)

    seat = (owner % N_X) * (seats // N_X) + owner // N_X
    spread = ((at((count, units), 0) // unit_rows) == at((count, units), 1)).astype(bf16)
    hot = (seat == at((units, seats), 1)).astype(bf16)
    pick_ref[...] = jnp.dot(spread, hot, preferred_element_type=f32).astype(bf16)
    lanes = at((units, head), 1)
    hot = (slot == (lanes % half) // unit_rows).astype(bf16)
    match = (at((count, head), 0) % unit_rows) == (at((count, head), 1) % unit_rows)
    hot = jnp.dot(spread, hot, preferred_element_type=f32)
    lane_ref[...] = jnp.where(match, hot, 0.0).astype(bf16)

    state = state_ref[...]
    high = state.astype(bf16)
    low = (state - high.astype(f32)).astype(bf16)
    copies = (at((unit_rows, head), 0) == at((unit_rows, head), 1) % unit_rows).astype(bf16)
    high = jnp.dot(high, copies, preferred_element_type=f32)
    low = jnp.dot(low, copies, preferred_element_type=f32)
    lanes = at((capacity, head), 1)
    parts = jnp.where(lanes < half, high, low)
    mine = (lanes % half) // unit_rows == at((capacity, head), 0)
    state_row = jnp.sum(jnp.where(mine, parts, 0.0), axis=0, keepdims=True)
    number = at((units, 1), 0)
    sums = jnp.zeros((units, 1), f32)
    for c in range(capacity):
        here = (owner == me) & (slot == c)
        total = jnp.sum(state[c : c + 1, :], axis=1, keepdims=True)
        sums = sums + jnp.where(here, total, 0.0)
        index_ref[c] = jnp.max(jnp.where(here, number.astype(f32), -1.0)).astype(jnp.int32)
    lanes = at((units, head), 1)
    tensor = at((units, head), 0) // unit_rows
    here = (lanes % tensors == tensor) & (lanes < 2 * tensors)
    value = jnp.sum(jnp.where(here, sums, 0.0), axis=0, keepdims=True)
    high = value.astype(bf16).astype(f32)
    sum_row = jnp.where(at((1, head), 1) < tensors, high, value - high)
    at_row = at(extra_ref.shape, 0)
    extra = jnp.where(at_row == row, state_row, jnp.where(at_row == row + 1, sum_row, 0.0))
    extra_ref[...] = extra.astype(bf16)


def tables(owner_table, state, head, seats, row, rows):
    capacity, unit_rows = state.shape
    count = owner_table.shape[0] * unit_rows
    vmem = pl.BlockSpec(memory_space=pltpu.VMEM)
    smem = pl.BlockSpec(memory_space=pltpu.SMEM)
    bf16 = jnp.bfloat16
    return pl.pallas_call(
        functools.partial(tables_kernel, row),
        out_shape=(
            jax.ShapeDtypeStruct((count, seats), bf16),
            jax.ShapeDtypeStruct((count, head), bf16),
            jax.ShapeDtypeStruct((rows, head), bf16),
            jax.ShapeDtypeStruct((capacity,), jnp.int32),
        ),
        in_specs=[vmem, vmem],
        out_specs=(vmem, vmem, vmem, smem),
        cost_estimate=pl.CostEstimate(
            flops=count * head * 100, bytes_accessed=4 * count * head, transcendentals=0
        ),
        compiler_params=pltpu.CompilerParams(vmem_limit_bytes=8 << 20),
        name="tables",
    )(owner_table, state)


def on_device(normed, cotangent, norm_gain, weights, row_state, col_state, owner_table):
    bf16, f32 = jnp.bfloat16, jnp.float32
    groups = lax.axis_size("grp")
    intra = lax.axis_size("intra")
    n_y = intra // CORES
    n_z = groups // N_X
    tensors, head = col_state.shape
    capacity, unit_rows = row_state.shape[2:]
    slab = weights.shape[0]
    blocks = slab // unit_rows
    units = tensors * blocks

    same_core = [[y * CORES + c for y in range(n_y)] for c in range(CORES)]
    x_groups = [[z * N_X + x for x in range(N_X)] for z in range(n_z)]
    z_groups = [[z * N_X + x for z in range(n_z)] for x in range(N_X)]


    swap = [(i, i ^ 1) for i in range(intra)]
    mine, theirs = arrange(normed, norm_gain[None, :], cotangent, slab)
    inputs = (mine, lax.ppermute(theirs, "intra", swap), cotangent, slab)
    n_pieces = mine.shape[1] // slab
    early = (0, 2)
    late = tuple(u for u in range(n_pieces) if u not in early)
    made = products(*inputs, early)
    made = made + products(*inputs, late, made[0])
    parts = [made[(early + late).index(u)] for u in range(n_pieces)]

    ring = [
        (y * CORES + c, ((y + 1 - 2 * c) % n_y) * CORES + c) for y in range(n_y) for c in range(CORES)
    ]

    def add(*terms):
        return sum(t.astype(f32) for t in terms)

    def hop(a):
        return lax.ppermute(a, "intra", ring)

    first, second = parts[0], parts[2]
    for k in range(1, len(parts) - 2, 2):
        first = add(hop(first), parts[k]).astype(bf16)
        if k > 1:
            second = add(hop(second), parts[k + 1]).astype(bf16)
    last = hop(first)
    give = add(hop(second), parts[-1]).astype(bf16)
    other = lax.ppermute(give, "intra", swap)
    state_rows = n_z + -n_z % unit_rows
    per_x = units // N_X
    full = per_x * unit_rows
    share = -(-full // (4 * n_z)) * 4
    sent_rows = -(-(share + 2) // unit_rows) * unit_rows
    pick, lane, extra, my_index = tables(
        owner_table, row_state[0, 0], head, N_X * state_rows, share, sent_rows
    )
    last, other, extra, pick, lane, my_index = lax.optimization_barrier(
        (last, other, extra, pick, lane, my_index)
    )
    own = finish(last, other, head)


    got = lax.all_to_all(own, "grp", 0, 0, axis_index_groups=x_groups, tiled=True)
    block = jax.ShapeDtypeStruct((n_z, sent_rows, head), bf16)
    sent = small_kernel(functools.partial(sum_x_kernel, share), block, got)
    got = lax.all_to_all(sent, "grp", 0, 0, axis_index_groups=z_groups, tiled=True)

    sent = small_kernel(sum_z_kernel, block, got, extra)
    got = lax.all_to_all(sent, "grp", 0, 0, axis_index_groups=z_groups, tiled=True)
    sent = jax.ShapeDtypeStruct((N_X, full + state_rows, head), bf16)
    sent = small_kernel(functools.partial(pack_kernel, share), sent, got)
    got = lax.all_to_all(sent, "grp", 0, 0, axis_index_groups=x_groups, tiled=True)

    stats = jax.ShapeDtypeStruct((2 * tensors, head), f32)
    stats = small_kernel(functools.partial(stats_kernel, n_z, full), stats, got)
    partner = lax.ppermute(stats, "intra", swap)
    shapes = (
        jax.ShapeDtypeStruct((units * unit_rows, head), f32),
        jax.ShapeDtypeStruct((capacity, unit_rows), f32),
    )
    scaled, row_moments = small_kernel(
        rows_kernel, shapes, my_index, row_state[0, 0], pick, lane, got, scalars=1
    )
    sent = jax.ShapeDtypeStruct((n_y,) + stats.shape, f32)
    sent = small_kernel(both_kernel, sent, stats, partner)
    stats = lax.all_to_all(sent, "intra", 0, 0, axis_index_groups=same_core, tiled=True)
    shapes = (
        jax.ShapeDtypeStruct(weights.shape, weights.dtype),
        jax.ShapeDtypeStruct(col_state.shape, f32),
    )
    new_weights, col_new = small_kernel(update_kernel, shapes, stats, scaled, weights, col_state)
    return (new_weights, row_moments[None, None], col_new)


def solution(mesh):
    placed = (
        P(("grp", "intra"), None),
        P(("grp", "intra"), None),
        P(),
        P("intra", None),
        P("grp", "intra", None, None),
        P(),
        P(),
    )
    return jax.shard_map(
        on_device,
        mesh=mesh,
        in_specs=placed,
        out_specs=(P("intra", None), P("grp", "intra", None, None), P()),
        check_vma=False,
    )
```

```python
import functools

import jax
import jax.numpy as jnp
from jax import lax
from jax.experimental import pallas as pl
from jax.experimental.pallas import tpu as pltpu
from jax.sharding import PartitionSpec as P


decay_rate = 0.8
step_size = 0.5
epsilon = 1e-06

N_X = 4
CORES = 2


def scale_pieces(slab, other, x_ref, gain_ref, out_ref):
    me = lax.axis_index("intra")
    my_y, my_core = me // CORES, me % CORES
    half = x_ref.shape[1] // (CORES * slab)
    n_y = 2 * half // CORES
    ahead = [n_y] + [2 * k + h for k in range(n_y // 2 - 1, 0, -1) for h in (0, 1)] + [1]
    behind = [n_y + 1] + [2 * k + h for k in range(n_y // 2 + 1, n_y) for h in (1, 0)] + [0]
    up, down = (behind, ahead) if other else (ahead, behind)
    for u in range(half):
        piece = lax.rem(jnp.where(my_core == 0, up[u], down[u]) + 2 * my_y, 2 * half)
        column = pl.multiple_of(piece * slab, slab)
        block = x_ref[:, pl.ds(column, slab)].astype(jnp.float32)
        scaled = block * gain_ref[:, pl.ds(column, slab)]
        out_ref[:, u * slab : (u + 1) * slab] = scaled.astype(out_ref.dtype)


def theirs_kernel(slab, x_hbm, gain_hbm, cot_hbm, out_ref, x_ref, gain_ref, cot_ref, sems):
    loads = [
        pltpu.make_async_copy(source, target, sems.at[n])
        for n, (source, target) in enumerate(
            ((x_hbm, x_ref), (gain_hbm, gain_ref), (cot_hbm, cot_ref))
        )
    ]
    for load in loads:
        load.start()
    for load in loads:
        load.wait()
    scale_pieces(slab, True, x_ref, gain_ref, out_ref)
    out_ref[:, x_ref.shape[1] // CORES :] = cot_ref[...]


def theirs_of(x, gain, cot, slab):
    tokens, d_model = x.shape
    return pl.pallas_call(
        functools.partial(theirs_kernel, slab),
        out_shape=jax.ShapeDtypeStruct((tokens, d_model // CORES + cot.shape[1]), x.dtype),
        in_specs=[pl.BlockSpec(memory_space=pltpu.HBM)] * 3,
        out_specs=pl.BlockSpec(memory_space=pltpu.VMEM),
        scratch_shapes=[
            pltpu.VMEM(x.shape, x.dtype),
            pltpu.VMEM(gain.shape, gain.dtype),
            pltpu.VMEM(cot.shape, cot.dtype),
            pltpu.SemaphoreType.DMA((3,)),
        ],
        cost_estimate=pl.CostEstimate(
            flops=tokens * d_model, bytes_accessed=4 * tokens * d_model, transcendentals=0
        ),
        compiler_params=pltpu.CompilerParams(vmem_limit_bytes=67000000),
        name="theirs",
    )(x, gain, cot)


def mine_kernel(slab, x_ref, gain_ref, after_ref, out_ref):
    scale_pieces(slab, False, x_ref, gain_ref, out_ref)


def mine_of(x, gain, slab, after):
    tokens, d_model = x.shape
    vmem = pl.BlockSpec(memory_space=pltpu.VMEM)
    return pl.pallas_call(
        functools.partial(mine_kernel, slab),
        out_shape=jax.ShapeDtypeStruct((tokens, d_model // CORES), x.dtype),
        in_specs=[vmem, vmem, pl.BlockSpec(memory_space=pl.ANY)],
        out_specs=vmem,
        cost_estimate=pl.CostEstimate(
            flops=tokens * d_model, bytes_accessed=2 * tokens * d_model, transcendentals=0
        ),
        compiler_params=pltpu.CompilerParams(vmem_limit_bytes=12 << 20),
        name="mine",
    )(x, gain, after)


def products_kernel(slab, pieces, after, x_ref, got_ref, c_ref, *outs):
    dims = (((0,), (0,)), ((), ()))
    rows = x_ref.shape[1]
    for u, out in zip(pieces, outs[after:]):
        cols = slice(u * slab, (u + 1) * slab)
        total = lax.dot_general(
            x_ref[:, cols], c_ref[...], dims, preferred_element_type=jnp.float32
        ) + lax.dot_general(
            got_ref[:, cols], got_ref[:, rows:], dims, preferred_element_type=jnp.float32
        )
        out[...] = total.astype(out.dtype)


def products(mine, got, cot, slab, pieces, *after):
    tokens = mine.shape[0]
    width = cot.shape[1]
    size = len(pieces) * slab * width
    vmem = pl.BlockSpec(memory_space=pltpu.VMEM)
    return pl.pallas_call(
        functools.partial(products_kernel, slab, pieces, len(after)),
        out_shape=tuple(jax.ShapeDtypeStruct((slab, width), cot.dtype) for _ in pieces),
        in_specs=[vmem] * 3 + [pl.BlockSpec(memory_space=pl.ANY)] * len(after),
        out_specs=tuple([vmem] * len(pieces)),
        cost_estimate=pl.CostEstimate(
            flops=4 * tokens * size, bytes_accessed=4 * size, transcendentals=0
        ),
        compiler_params=pltpu.CompilerParams(vmem_limit_bytes=16 << 20),
        name="products",
    )(mine, got, cot, *after)


def finish_kernel(a_ref, b_ref, out_ref):
    head = out_ref.shape[2]
    slab = a_ref.shape[0]
    for t in range(a_ref.shape[1] // head):
        cols = slice(t * head, (t + 1) * head)
        total = a_ref[:, cols].astype(jnp.float32) + b_ref[:, cols].astype(jnp.float32)
        x, row = divmod(t * slab, out_ref.shape[1])
        out_ref[x, row : row + slab, :] = total.astype(out_ref.dtype)


def finish(a, b, head):
    vmem = pl.BlockSpec(memory_space=pltpu.VMEM)
    return pl.pallas_call(
        finish_kernel,
        out_shape=jax.ShapeDtypeStruct((N_X, a.size // (N_X * head), head), a.dtype),
        in_specs=[vmem, vmem],
        out_specs=vmem,
        cost_estimate=pl.CostEstimate(
            flops=a.size, bytes_accessed=6 * a.size, transcendentals=0
        ),
        compiler_params=pltpu.CompilerParams(vmem_limit_bytes=8 << 20),
        name="finish",
    )(a, b)


def small_kernel(body, out_shape, *operands, scalars=0):
    vmem = pl.BlockSpec(memory_space=pltpu.VMEM)
    smem = pl.BlockSpec(memory_space=pltpu.SMEM)
    size = sum(a.size for a in operands)
    return pl.pallas_call(
        body,
        out_shape=out_shape,
        in_specs=[smem] * scalars + [vmem] * (len(operands) - scalars),
        out_specs=jax.tree.map(lambda _: vmem, out_shape),
        cost_estimate=pl.CostEstimate(flops=size, bytes_accessed=4 * size, transcendentals=0),
        compiler_params=pltpu.CompilerParams(vmem_limit_bytes=8 << 20),
    )(*operands)


def total_of(ref, rows=slice(None)):
    return sum(ref[j, rows, :].astype(jnp.float32) for j in range(ref.shape[0]))


def sum_x_kernel(rows, got_ref, out_ref):
    total = total_of(got_ref)
    full, head = total.shape
    for j in range(out_ref.shape[0]):
        begin, end = min(j * rows, full), min(j * rows + rows, full)
        fill = jnp.zeros((out_ref.shape[1] - end + begin, head), jnp.float32)
        block = jnp.concatenate([total[begin:end], fill], axis=0)
        out_ref[j] = block.astype(out_ref.dtype)


def sum_z_kernel(got_ref, extra_ref, out_ref):
    total = total_of(got_ref) + extra_ref[...].astype(jnp.float32)
    for j in range(out_ref.shape[0]):
        out_ref[j] = total.astype(out_ref.dtype)


def pack_kernel(rows, got_ref, out_ref):
    count, _, head = got_ref.shape
    pad = -count % 16
    full = out_ref.shape[1] - count - pad
    blocks = [got_ref[j].astype(jnp.float32) for j in range(count)]
    grad = jnp.concatenate([block[:rows] for block in blocks], axis=0)[:full]
    grad = grad.astype(out_ref.dtype)
    sums = sum(block[rows + 1 : rows + 2] for block in blocks)
    high = sums.astype(out_ref.dtype).astype(jnp.float32)
    tail = [block[rows : rows + 1] for block in blocks] + [high, sums - high]
    tail = jnp.concatenate(tail + [jnp.zeros((pad - 2, head), jnp.float32)], axis=0)
    for x in range(out_ref.shape[0]):
        out_ref[x, :full, :] = grad
        out_ref[x, full:, :] = tail.astype(out_ref.dtype)


def stats_kernel(count, full, got_ref, out_ref):
    half = full // 2
    rows = []
    for x in range(got_ref.shape[0]):
        for t in range(2):
            grad = got_ref[x, t * half : (t + 1) * half, :].astype(jnp.float32)
            rows.append(jnp.sum(grad * grad, axis=0, keepdims=True))
    tails = [got_ref[x, full:, :].astype(jnp.float32) for x in range(got_ref.shape[0])]
    rows.append(sum(t[count : count + 1] + t[count + 1 : count + 2] for t in tails))
    fill = out_ref.shape[0] - len(rows)
    rows.append(jnp.zeros((fill, out_ref.shape[1]), jnp.float32))
    out_ref[...] = jnp.concatenate(rows, axis=0)


def both_kernel(a_ref, b_ref, out_ref):
    total = a_ref[...] + b_ref[...]
    for j in range(out_ref.shape[0]):
        out_ref[j] = total


def rows_kernel(index_ref, state_ref, pick_ref, lane_ref, got_ref, out_ref, own_ref):
    n_x, _, head = got_ref.shape
    full = pick_ref.shape[0] // n_x
    slab = full // 2
    states = jnp.concatenate([got_ref[x, full:, :] for x in range(n_x)], axis=0)
    for t in range(2 * n_x):
        grad = got_ref[t // 2, (t % 2) * slab : (t % 2 + 1) * slab, :].astype(jnp.float32)
        where = slice(t * slab, (t + 1) * slab)
        state = jnp.dot(pick_ref[where, :], states, preferred_element_type=jnp.float32)
        prev = jnp.sum(state * lane_ref[where, :].astype(jnp.float32), axis=1, keepdims=True)
        mean = jnp.sum(grad * grad, axis=1, keepdims=True) / head + epsilon
        out_ref[where, :] = grad * lax.rsqrt(decay_rate * prev + (1.0 - decay_rate) * mean)

    capacity, unit_rows = own_ref.shape
    per_piece = full // unit_rows
    shape = (unit_rows, unit_rows)
    eye = lax.broadcasted_iota(jnp.int32, shape, 0) == lax.broadcasted_iota(jnp.int32, shape, 1)
    for c in range(capacity):
        unit = jnp.maximum(index_ref[c], 0)
        rows = pl.ds(pl.multiple_of((unit % per_piece) * unit_rows, unit_rows), unit_rows)
        grad = got_ref[0, rows, :]
        for x in range(1, n_x):
            grad = jnp.where(unit // per_piece == x, got_ref[x, rows, :], grad)
        grad = grad.astype(jnp.float32)
        mean = jnp.sum(grad * grad, axis=1, keepdims=True) / head + epsilon
        mean = jnp.sum(jnp.where(eye, mean, 0.0), axis=0, keepdims=True)
        new = decay_rate * state_ref[c : c + 1, :] + (1.0 - decay_rate) * mean
        own_ref[c : c + 1, :] = jnp.where(index_ref[c] >= 0, new, 0.0)


def update_kernel(stats_ref, grad_ref, weight_ref, state_ref, out_ref, col_ref):
    tensors, head = state_ref.shape
    slab = weight_ref.shape[0]
    d_model = CORES * slab * stats_ref.shape[0]
    total = sum(stats_ref[j] for j in range(stats_ref.shape[0])) / d_model
    for t in range(tensors):
        col = total[t : t + 1] + epsilon
        col_new = decay_rate * state_ref[t : t + 1, :] + (1.0 - decay_rate) * col
        col_ref[t : t + 1, :] = col_new
        sums = total[tensors : tensors + 1]
        prev = sums[:, t : t + 1] + sums[:, tensors + t : tensors + t + 1]
        average = decay_rate * prev + (1.0 - decay_rate) * jnp.mean(col, axis=1, keepdims=True)
        factor = step_size * lax.rsqrt(col_new / average)
        cols = slice(t * head, (t + 1) * head)
        change = grad_ref[t * slab : (t + 1) * slab, :] * factor
        out_ref[:, cols] = (weight_ref[:, cols].astype(jnp.float32) - change).astype(out_ref.dtype)


def tables_kernel(row, owner_ref, state_ref, pick_ref, lane_ref, extra_ref, index_ref):
    f32, bf16 = jnp.float32, jnp.bfloat16
    me = lax.axis_index("grp")
    units = owner_ref.shape[0]
    capacity, unit_rows = state_ref.shape
    count, head = lane_ref.shape
    half = capacity * unit_rows
    tensors = units // unit_rows
    seats = pick_ref.shape[1]

    def at(shape, axis):
        return lax.broadcasted_iota(jnp.int32, shape, axis)

    owner = owner_ref[...]
    hot = (owner == at((units, head), 1)).astype(f32)
    earlier = (at((units, units), 1) < at((units, units), 0)).astype(bf16)
    before = jnp.dot(earlier, hot.astype(bf16), preferred_element_type=f32)
    slot = jnp.sum(before * hot, axis=1, keepdims=True).astype(jnp.int32)

    seat = (owner % N_X) * (seats // N_X) + owner // N_X
    spread = ((at((count, units), 0) // unit_rows) == at((count, units), 1)).astype(bf16)
    hot = (seat == at((units, seats), 1)).astype(bf16)
    pick_ref[...] = jnp.dot(spread, hot, preferred_element_type=f32).astype(bf16)
    lanes = at((units, head), 1)
    hot = (slot == (lanes % half) // unit_rows).astype(bf16)
    match = (at((count, head), 0) % unit_rows) == (at((count, head), 1) % unit_rows)
    hot = jnp.dot(spread, hot, preferred_element_type=f32)
    lane_ref[...] = jnp.where(match, hot, 0.0).astype(bf16)

    state = state_ref[...]
    high = state.astype(bf16)
    low = (state - high.astype(f32)).astype(bf16)
    copies = (at((unit_rows, head), 0) == at((unit_rows, head), 1) % unit_rows).astype(bf16)
    high = jnp.dot(high, copies, preferred_element_type=f32)
    low = jnp.dot(low, copies, preferred_element_type=f32)
    lanes = at((capacity, head), 1)
    parts = jnp.where(lanes < half, high, low)
    mine = (lanes % half) // unit_rows == at((capacity, head), 0)
    state_row = jnp.sum(jnp.where(mine, parts, 0.0), axis=0, keepdims=True)
    number = at((units, 1), 0)
    sums = jnp.zeros((units, 1), f32)
    for c in range(capacity):
        here = (owner == me) & (slot == c)
        total = jnp.sum(state[c : c + 1, :], axis=1, keepdims=True)
        sums = sums + jnp.where(here, total, 0.0)
        index_ref[c] = jnp.max(jnp.where(here, number.astype(f32), -1.0)).astype(jnp.int32)
    lanes = at((units, head), 1)
    tensor = at((units, head), 0) // unit_rows
    here = (lanes % tensors == tensor) & (lanes < 2 * tensors)
    value = jnp.sum(jnp.where(here, sums, 0.0), axis=0, keepdims=True)
    high = value.astype(bf16).astype(f32)
    sum_row = jnp.where(at((1, head), 1) < tensors, high, value - high)
    at_row = at(extra_ref.shape, 0)
    extra = jnp.where(at_row == row, state_row, jnp.where(at_row == row + 1, sum_row, 0.0))
    extra_ref[...] = extra.astype(bf16)


def tables(owner_table, state, head, seats, row, rows):
    capacity, unit_rows = state.shape
    count = owner_table.shape[0] * unit_rows
    vmem = pl.BlockSpec(memory_space=pltpu.VMEM)
    smem = pl.BlockSpec(memory_space=pltpu.SMEM)
    bf16 = jnp.bfloat16
    return pl.pallas_call(
        functools.partial(tables_kernel, row),
        out_shape=(
            jax.ShapeDtypeStruct((count, seats), bf16),
            jax.ShapeDtypeStruct((count, head), bf16),
            jax.ShapeDtypeStruct((rows, head), bf16),
            jax.ShapeDtypeStruct((capacity,), jnp.int32),
        ),
        in_specs=[vmem, vmem],
        out_specs=(vmem, vmem, vmem, smem),
        cost_estimate=pl.CostEstimate(
            flops=count * head * 100, bytes_accessed=4 * count * head, transcendentals=0
        ),
        compiler_params=pltpu.CompilerParams(vmem_limit_bytes=8 << 20),
        name="tables",
    )(owner_table, state)


def on_device(normed, cotangent, norm_gain, weights, row_state, col_state, owner_table):
    bf16, f32 = jnp.bfloat16, jnp.float32
    groups = lax.axis_size("grp")
    intra = lax.axis_size("intra")
    n_y = intra // CORES
    n_z = groups // N_X
    tensors, head = col_state.shape
    capacity, unit_rows = row_state.shape[2:]
    slab = weights.shape[0]
    blocks = slab // unit_rows
    units = tensors * blocks

    same_core = [[y * CORES + c for y in range(n_y)] for c in range(CORES)]
    x_groups = [[z * N_X + x for x in range(N_X)] for z in range(n_z)]
    z_groups = [[z * N_X + x for z in range(n_z)] for x in range(N_X)]


    swap = [(i, i ^ 1) for i in range(intra)]
    gain = norm_gain[None, :]
    theirs = theirs_of(normed, gain, cotangent, slab)
    mine = mine_of(normed, gain, slab, theirs)
    inputs = (mine, lax.ppermute(theirs, "intra", swap), cotangent, slab)
    n_pieces = mine.shape[1] // slab
    early = (0, 2)
    late = tuple(u for u in range(n_pieces) if u not in early)
    made = products(*inputs, early)
    made = made + products(*inputs, late, made[0])
    parts = [made[(early + late).index(u)] for u in range(n_pieces)]

    ring = [
        (y * CORES + c, ((y + 1 - 2 * c) % n_y) * CORES + c) for y in range(n_y) for c in range(CORES)
    ]

    def add(*terms):
        return sum(t.astype(f32) for t in terms)

    def hop(a):
        return lax.ppermute(a, "intra", ring)

    first, second = parts[0], parts[2]
    for k in range(1, len(parts) - 2, 2):
        first = add(hop(first), parts[k]).astype(bf16)
        if k > 1:
            second = add(hop(second), parts[k + 1]).astype(bf16)
    last = hop(first)
    give = add(hop(second), parts[-1]).astype(bf16)
    other = lax.ppermute(give, "intra", swap)
    state_rows = n_z + -n_z % unit_rows
    per_x = units // N_X
    full = per_x * unit_rows
    share = -(-full // (4 * n_z)) * 4
    sent_rows = -(-(share + 2) // unit_rows) * unit_rows
    pick, lane, extra, my_index = tables(
        owner_table, row_state[0, 0], head, N_X * state_rows, share, sent_rows
    )
    last, other, extra, pick, lane, my_index = lax.optimization_barrier(
        (last, other, extra, pick, lane, my_index)
    )
    own = finish(last, other, head)


    got = lax.all_to_all(own, "grp", 0, 0, axis_index_groups=x_groups, tiled=True)
    block = jax.ShapeDtypeStruct((n_z, sent_rows, head), bf16)
    sent = small_kernel(functools.partial(sum_x_kernel, share), block, got)
    got = lax.all_to_all(sent, "grp", 0, 0, axis_index_groups=z_groups, tiled=True)

    sent = small_kernel(sum_z_kernel, block, got, extra)
    got = lax.all_to_all(sent, "grp", 0, 0, axis_index_groups=z_groups, tiled=True)
    sent = jax.ShapeDtypeStruct((N_X, full + state_rows, head), bf16)
    sent = small_kernel(functools.partial(pack_kernel, share), sent, got)
    got = lax.all_to_all(sent, "grp", 0, 0, axis_index_groups=x_groups, tiled=True)

    stats = jax.ShapeDtypeStruct((2 * tensors, head), f32)
    stats = small_kernel(functools.partial(stats_kernel, n_z, full), stats, got)
    partner = lax.ppermute(stats, "intra", swap)
    shapes = (
        jax.ShapeDtypeStruct((units * unit_rows, head), f32),
        jax.ShapeDtypeStruct((capacity, unit_rows), f32),
    )
    scaled, row_moments = small_kernel(
        rows_kernel, shapes, my_index, row_state[0, 0], pick, lane, got, scalars=1
    )
    sent = jax.ShapeDtypeStruct((n_y,) + stats.shape, f32)
    sent = small_kernel(both_kernel, sent, stats, partner)
    stats = lax.all_to_all(sent, "intra", 0, 0, axis_index_groups=same_core, tiled=True)
    shapes = (
        jax.ShapeDtypeStruct(weights.shape, weights.dtype),
        jax.ShapeDtypeStruct(col_state.shape, f32),
    )
    new_weights, col_new = small_kernel(update_kernel, shapes, stats, scaled, weights, col_state)
    return (new_weights, row_moments[None, None], col_new)


def solution(mesh):
    placed = (
        P(("grp", "intra"), None),
        P(("grp", "intra"), None),
        P(),
        P("intra", None),
        P("grp", "intra", None, None),
        P(),
        P(),
    )
    return jax.shard_map(
        on_device,
        mesh=mesh,
        in_specs=placed,
        out_specs=(P("intra", None), P("grp", "intra", None, None), P()),
        check_vma=False,
    )
```
